32 devices in a mesh: parts: 2 (over x), ctx: 16 (over z, y, core).
Axes of the slice: x: 2, y: 2, z: 4, core: 2. Of those that a mesh axis runs over, the one named last changes fastest.
Arguments:
- values: bfloat16 [4096, 2048], P(('parts', 'ctx')), parts along dimension 0, may hold values from -6 to 6
- gating: bfloat16 [4096, 2048], P(('parts', 'ctx')), parts along dimension 0, may hold values from -6 to 6
- out_weight: bfloat16 [4096, 2048], P(('parts', 'ctx')), parts along dimension 0, may hold values from -0.125 to 0.125
- residue: float32 [4096, 64], P('parts'), parts along dimension 0, may hold values from -0.03125 to 0.03125
- decay_rate: float32 [32, 64], P('parts'), parts along dimension 0, may hold values from 0.2 to 400
- skip_gain: float32 [4096], P('parts'), parts along dimension 0, may hold values from 0.5 to 1.5
- cotangent: bfloat16 [4096, 2048], P(('parts', 'ctx')), parts along dimension 0, may hold values from -6 to 6
Outputs:
- output: bfloat16 [4096, 2048], P(('parts', 'ctx')), parts along dimension 0
- value_grad: bfloat16 [4096, 2048], P(('parts', 'ctx')), parts along dimension 0
- gate_grad: bfloat16 [4096, 2048], P(('parts', 'ctx')), parts along dimension 0
- weight_grad: float32 [4096, 2048], P(('parts', 'ctx')), parts along dimension 0
The draws below stay inside these ranges and needn't reach their ends.
There are 2 independent parts, one for each index of `parts`. The reference program is written for one: setup_inputs(seed, part) draws one part's arguments, and reference() takes and returns one part's arrays. A program takes and returns all parts, laid end to end along the dimension named above; each array names one. Nothing has to cross between parts.
All inputs are finite; a program needn't handle non-finite values.
Results may differ from the reference program's by a relative error of at most 0.0049.
Values may be sent and summed in bfloat16 or wider, within the bound.
No kernel may reach another device: no remote copies, remote signals or barrier semaphores. Data moves between devices by JAX's collectives and lax.ppermute only.
A program may use at most 192 MiB of HBM per device.

```python
import math
import jax
import jax.numpy as jnp
from jax import lax

D = 2048
GROUPS = 16
MODES = 64
SEQ = 2048


def shard_levels(stream_key, dims, pieces, least, high):
    def one(axis_at, shards_of):
        heights = jax.random.uniform(jax.random.fold_in(jax.random.fold_in(stream_key, 6), axis_at), (shards_of,), jnp.float32, least / len(pieces), high / len(pieces))
        return jnp.repeat(jnp.exp(heights), dims[axis_at] // shards_of).reshape((-1,) + (1,) * (len(dims) - axis_at - 1))

    gain = one(*pieces[0])
    for cut in pieces[1:]:
        gain = gain * one(*cut)
    return gain


def noise(key, extent, spread, reach, pieces=(), kind=jnp.bfloat16):
    values = spread * jax.random.normal(key, extent, jnp.float32)
    if pieces:
        values = values * shard_levels(key, extent, pieces, -0.22, 0.18)
    return jnp.clip(values, -reach, reach).astype(kind)


def setup_inputs(seed: int = 0, part: int = 0) -> dict:
    streams_of = jax.random.split(jax.random.key(seed), 8)
    own_keys = jax.random.split(jax.random.fold_in(streams_of[7], part), 8)
    values = noise(own_keys[0], (SEQ, D), 1.0, 6.0, ((0, 16),))
    gating = noise(own_keys[1], (SEQ, D), 1.0, 6.0, ((0, 16),))
    out_weight = noise(own_keys[2], (D, D), D ** -0.5, 0.125, ((0, 16),))
    residue = noise(own_keys[3], (D, MODES), (20 * SEQ) ** -0.5, 0.03125, (), jnp.float32)
    decay_rate = jnp.clip(jnp.exp(jax.random.uniform(own_keys[4], (GROUPS, MODES), jnp.float32, math.log(0.2), math.log(400.0))), 0.2, 400.0)
    skip_gain = jnp.clip(1.0 + 0.1 * jax.random.normal(own_keys[5], (D,), jnp.float32), 0.5, 1.5)
    cotangent = noise(own_keys[6], (SEQ, D), 1.0, 6.0, ((0, 16),))
    return {"values": values, "gating": gating, "out_weight": out_weight, "residue": residue, "decay_rate": decay_rate, "skip_gain": skip_gain, "cotangent": cotangent}


def tap_table(residue, decay_rate):
    channels = D // GROUPS
    lag_axis = jnp.arange(SEQ).astype(jnp.float32)

    def one_group(pair):
        res_group, rate_group = pair
        powers = jnp.exp(-lag_axis[:, None] * (rate_group[None, :] / SEQ))
        return jnp.dot(powers, res_group.T, precision=lax.Precision.HIGHEST)

    return lax.map(one_group, (residue.reshape(GROUPS, channels, MODES), decay_rate))


def causal_conv(tables, signal):
    channels = D // GROUPS
    grouped = signal.reshape(SEQ, GROUPS, channels).transpose(1, 0, 2)

    def one_group(pair):
        taps, piece = pair
        length = 2 * SEQ
        spectrum = jnp.fft.rfft(taps, n=length, axis=0) * jnp.fft.rfft(piece, n=length, axis=0)
        return jnp.fft.irfft(spectrum, n=length, axis=0)[:SEQ]

    result = lax.map(one_group, (tables, grouped))
    return result.transpose(1, 0, 2).reshape(SEQ, D)


def reference(values, gating, out_weight, residue, decay_rate, skip_gain, cotangent):
    tables = tap_table(residue, decay_rate)
    signal = values.astype(jnp.float32)
    gate_float = gating.astype(jnp.float32)
    conv = causal_conv(tables, signal) + skip_gain[None, :] * signal
    mixed = (gate_float * conv).astype(jnp.bfloat16)
    output = jnp.dot(mixed, out_weight, preferred_element_type=jnp.float32).astype(jnp.bfloat16)
    mixed_grad = jnp.dot(cotangent, out_weight.T, preferred_element_type=jnp.float32)
    gate_grad = (mixed_grad * conv).astype(jnp.bfloat16)
    signal_back = mixed_grad * gate_float
    anti = causal_conv(tables, signal_back[::-1])[::-1] + skip_gain[None, :] * signal_back
    value_grad = anti.astype(jnp.bfloat16)
    weight_grad = jnp.dot(mixed.T, cotangent, preferred_element_type=jnp.float32)
    return (output, value_grad, gate_grad, weight_grad)
```

```python
import functools

import jax
import jax.numpy as jnp
from jax import lax
from jax.experimental import pallas as pl
from jax.experimental.pallas import tpu as pltpu
from jax.sharding import PartitionSpec as P

SUB = 16
LANES = 4
BF16 = jnp.bfloat16
F32 = jnp.float32
VMEM_LIMIT = 56 * 1024 * 1024


def split(a):
    high = a.astype(BF16)
    return high, (a - high.astype(F32)).astype(BF16)


def dot(a, b, dims=((1,), (0,))):
    return lax.dot_general(a, b, (dims, ((), ())), preferred_element_type=F32)


def dot3(a_high, a_low, b):
    b_high, b_low = split(b)
    return dot(a_high, b_high) + dot(a_low, b_high) + dot(a_high, b_low)


def beside(parts):
    return jnp.concatenate(parts, axis=1)


def call(body, grid, in_specs, out_specs, out_shape, scratch=(), flops=0, moved=0, scalars=1, name=None):
    return pl.pallas_call(
        body,
        grid_spec=pltpu.PrefetchScalarGridSpec(
            num_scalar_prefetch=scalars,
            grid=grid,
            in_specs=in_specs,
            out_specs=out_specs,
            scratch_shapes=list(scratch),
        ),
        out_shape=out_shape,
        compiler_params=pltpu.CompilerParams(vmem_limit_bytes=VMEM_LIMIT),
        cost_estimate=pl.CostEstimate(flops=flops, bytes_accessed=moved, transcendentals=0),
        name=name,
    )


def whole(shape):
    return pl.BlockSpec(shape, lambda *_: (0,) * len(shape))


def block(shape, at=None):
    if at is None:
        return pl.BlockSpec((1,) + shape, lambda i, *_: (i,) + (0,) * len(shape))
    return pl.BlockSpec((1,) + shape, lambda *_: (at,) + (0,) * len(shape))


def powers_kernel(rate_col, rate_row, res, af_h, af_l, ab_h, ab_l, lf_h, lf_l, lb_h, lb_l, taps, *, tokens, modes):
    subs = tokens // SUB
    depth = subs * modes
    row = lax.broadcasted_iota(jnp.int32, (depth, tokens), 0) // modes
    tok = lax.broadcasted_iota(jnp.int32, (depth, tokens), 1)

    def power(steps, rate, valid):
        held = jnp.maximum(steps, 0).astype(F32)
        return jnp.where(valid, jnp.exp(-held * rate), 0.0)

    rc = rate_col[0]
    ahead = SUB * (row + 1) - 1 - tok
    af_h[0], af_l[0] = split(power(ahead, rc, ahead >= 0))
    behind = tok - SUB * row
    ab_h[0], ab_l[0] = split(power(behind, rc, behind >= 0))
    col = lax.broadcasted_iota(jnp.int32, (tokens, depth), 1) // modes
    out = lax.broadcasted_iota(jnp.int32, (tokens, depth), 0)
    inside = out % SUB
    rr = rate_row[0]
    carry = col == subs - 1
    steps = jnp.where(carry, out + 1, inside + 1)
    lf_h[0], lf_l[0] = split(power(steps, rr, carry | (out // SUB == col + 1)))
    carry = col == 0
    steps = jnp.where(carry, tokens - out, SUB - inside)
    lb_h[0], lb_l[0] = split(power(steps, rr, carry | (out // SUB == col - 1)))
    lag = lax.broadcasted_iota(jnp.int32, (SUB, modes), 0).astype(F32)
    taps[0] = lax.dot_general(
        jnp.exp(-lag * rr[:, :modes]),
        res[0],
        (((1,), (0,)), ((), ())),
        precision=lax.Precision.HIGHEST,
        preferred_element_type=F32,
    )


def inner_conv(xs, x_scr, e_scr, c_scr, inner, end, a_h, a_l, l_h, l_l, taps, res, rate_col, skip, lane, exact, back):
    tokens, width = xs[0].shape
    modes = res.shape[0]
    subs = tokens // SUB
    order = range(LANES - 1, -1, -1) if back else range(LANES)
    joined = width % 128 == 0
    groups = [list(range(LANES))] if joined else [[s] for s in range(LANES)]
    starts = [None] * LANES
    for group in groups:
        x = beside([xs[s] for s in group]) if len(group) > 1 else xs[group[0]]
        if exact:
            xh = x.astype(BF16)
            st = dot(a_h, xh) + dot(a_l, xh)
        else:
            st = dot3(a_h, a_l, x)
        for at, s in enumerate(group):
            starts[s] = st[:, at * width : (at + 1) * width]
    for s in range(LANES):
        part = starts[s]
        e_scr[s ^ lane] = part[:modes] if back else part[(subs - 1) * modes :]
    fade = jnp.exp(-float(tokens) * rate_col)
    state = jnp.zeros((modes, width), F32)
    for k in order:
        c_scr[k] = state
        state = fade * state + e_scr[k]
    end[...] = state
    weight = jnp.concatenate([res] * subs, axis=0)
    for group in groups:
        pieces = []
        for s in group:
            c = c_scr[s ^ lane]
            if back:
                full = jnp.concatenate([c, starts[s][modes:]], axis=0)
            else:
                full = jnp.concatenate([starts[s][: (subs - 1) * modes], c], axis=0)
            pieces.append(full * weight)
        w = beside(pieces) if len(pieces) > 1 else pieces[0]
        cross = dot3(l_h, l_l, w)
        for at, s in enumerate(group):
            inner[pl.ds(s * tokens, tokens), :] = cross[:, at * width : (at + 1) * width]
    row = lax.broadcasted_iota(jnp.int32, (SUB, width), 0)
    tap = taps + jnp.where(row == 0, skip, 0.0)
    spread = [jnp.broadcast_to(tap[k : k + 1, :], (subs, width)) for k in range(SUB)]
    for s in range(LANES):
        x_scr[...] = xs[s]
        held = [x_scr[pl.ds(t, subs, stride=SUB), :] for t in range(SUB)]
        for t in range(SUB):
            sources = range(t, SUB) if back else range(t + 1)
            total = None
            for u in sources:
                term = spread[abs(t - u)] * held[u]
                total = term if total is None else total + term
            at = pl.ds(s * tokens + t, subs, stride=SUB)
            inner[at, :] = inner[at, :] + total


def entering(coming, rate_col, span):
    total = None
    for hop, state in enumerate(coming):
        term = state if hop == 0 else jnp.exp(-float(span * hop) * rate_col) * state
        total = term if total is None else total + term
    return total


def cross_conv(state, lead_h, lead_l, res, rate_col, lane, tokens, back):
    width = state.shape[1]
    weighted = state * res
    joined = width % 128 == 0
    parts = []
    for s in range(LANES):
        k = s ^ lane
        steps = ((LANES - 1 - k) if back else k).astype(F32) * float(tokens)
        parts.append(jnp.exp(-steps * rate_col) * weighted)
    if joined:
        cross = dot3(lead_h, lead_l, beside(parts))
        return [cross[:, s * width : (s + 1) * width] for s in range(LANES)]
    return [dot3(lead_h, lead_l, p) for p in parts]


def forward_kernel(place, *refs):
    xs = refs[:LANES]
    a_h, a_l, l_h, l_l, taps, res, rate_col, skip, inner, end, x_scr, e_scr, c_scr = refs[LANES:]
    modes = res.shape[1]
    inner_conv(
        [x[0].astype(F32) for x in xs], x_scr, e_scr, c_scr, inner.at[0], end.at[0],
        a_h[0], a_l[0], l_h[0], l_l[0], taps[0], res[0], rate_col[0][:modes], skip[0], place[0], True, False,
    )


def mixed_kernel(place, *refs, hops):
    coming, refs = refs[:hops], refs[hops:]
    gates, refs = refs[:LANES], refs[LANES:]
    cots, refs = refs[:LANES], refs[LANES:]
    inner, l_h, l_l, res, rate_col, conv, mixed, wgrad = refs
    tokens = gates[0].shape[1]
    modes = res.shape[1]
    rate = rate_col[0][:modes]
    state = entering([c[0] for c in coming], rate, LANES * tokens)
    depth = l_h.shape[2]
    parts = cross_conv(
        state, l_h[0][:, depth - modes :], l_l[0][:, depth - modes :], res[0], rate, place[0], tokens, False
    )
    rounded = []
    for s in range(LANES):
        at = pl.ds(s * tokens, tokens)
        value = inner[0, at, :] + parts[s]
        conv[at, :] = value
        product = (gates[s][0].astype(F32) * value).astype(BF16)
        mixed[at, :] = product
        rounded.append(product)
    left = jnp.concatenate(rounded, axis=0)
    columns = wgrad.shape[1]
    tile = min(512, columns)
    for c in range(0, columns, tile):
        right = jnp.concatenate([cot[:, c : c + tile] for cot in cots], axis=0)
        wgrad[:, c : c + tile] = dot(left, right, ((0,), (0,))).astype(wgrad.dtype)


def backward_kernel(place, *refs):
    w0, w1, refs = refs[0], refs[1], refs[2:]
    gates, refs = refs[:LANES], refs[LANES:]
    cots, refs = refs[:LANES], refs[LANES:]
    conv, a_h, a_l, l_h, l_l, taps, res, rate_col, skip = refs[:9]
    ggrads = refs[9 : 9 + LANES]
    inner, end, x_scr, e_scr, c_scr = refs[9 + LANES :]
    modes = res.shape[1]
    tokens = gates[0].shape[1]
    weight = jnp.concatenate([w0[...], w1[...]], axis=0)
    backs = []
    for s in range(LANES):
        grad = dot(cots[s][...], weight, ((1,), (1,)))
        ggrads[s][...] = (grad * conv[pl.ds(s * tokens, tokens), :]).astype(BF16)
        backs.append(grad * gates[s][0].astype(F32))
    inner_conv(
        backs, x_scr, e_scr, c_scr, inner, end,
        a_h[0], a_l[0], l_h[0], l_l[0], taps[0], res[0], rate_col[0][:modes], skip[0], place[0], False, True,
    )


def value_kernel(place, *refs, hops):
    coming, refs = refs[:hops], refs[hops:]
    inner, l_h, l_l, res, rate_col = refs[:5]
    outs = refs[5:]
    tokens = outs[0].shape[0]
    modes = res.shape[1]
    rate = rate_col[0][:modes]
    state = entering([c[0] for c in coming], rate, LANES * tokens)
    parts = cross_conv(state, l_h[0][:, :modes], l_l[0][:, :modes], res[0], rate, place[0], tokens, True)
    for s in range(LANES):
        outs[s][...] = (inner[pl.ds(s * tokens, tokens), :] + parts[s]).astype(BF16)


def output_kernel(place, *refs, blocks):
    mixeds, refs = refs[:blocks], refs[blocks:]
    weights, outs = refs[: 2 * blocks], refs[2 * blocks :]
    tokens = outs[0].shape[0]
    width = mixeds[0].shape[1]
    if width % 128 == 0:
        left = beside([m[...] for m in mixeds])
        right = jnp.concatenate([w[...] for w in weights], axis=0)
        total = dot(left, right)
    else:
        total = 0.0
        for b in range(blocks):
            right = jnp.concatenate([weights[2 * b][...], weights[2 * b + 1][...]], axis=0)
            total = total + dot(mixeds[b][...], right)
    for s in range(LANES):
        outs[s][...] = total[s * tokens : (s + 1) * tokens].astype(outs[s].dtype)


def pack_kernel(place, x, *outs, blocks, width):
    lane, turn = place[0], place[1]
    for s in range(LANES):
        for m in range(blocks):
            at = lax.rem(turn - m + blocks, blocks) * LANES + (s ^ lane)
            outs[s][m] = x[:, pl.ds(pl.multiple_of(at * width, width), width)]


def unpack_kernel(place, *refs, blocks, width):
    lane, turn = place[0], place[1]
    outs = refs[-2:]
    for which in range(2):
        for s in range(LANES):
            for m in range(blocks):
                piece = refs[(which * LANES + s) * blocks + m]
                at = lax.rem(turn - m + blocks, blocks) * LANES + (s ^ lane)
                outs[which][:, pl.ds(pl.multiple_of(at * width, width), width)] = piece[...]


def per_device(values, gating, out_weight, residue, decay_rate, skip_gain, cotangent):
    tokens, width = values.shape
    groups, modes = decay_rate.shape
    count = lax.axis_size("ctx")
    blocks = count // LANES
    cw = width // count
    span = LANES * tokens
    rows = out_weight.shape[0]
    subs = tokens // SUB
    depth = subs * modes
    me = lax.axis_index("ctx")
    lane, turn = lax.rem(me, LANES), me // LANES
    place = jnp.stack([lane, turn]).astype(jnp.int32)

    def swap(x, s):
        return lax.ppermute(x, "ctx", [(i, i ^ s) for i in range(count)])

    def shift(x, hop, wrap):
        pairs = []
        for i in range(count):
            to = i + hop * LANES
            if wrap:
                pairs.append((i, to % count))
            elif 0 <= to < count:
                pairs.append((i, to))
        return lax.ppermute(x, "ctx", pairs)

    f32 = lambda *s: jax.ShapeDtypeStruct(s, F32)
    b16 = lambda *s: jax.ShapeDtypeStruct(s, BF16)

    slots = [lax.rem(turn - m + blocks, blocks) for m in range(blocks)]

    def pack(x):
        if cw % 128 == 0:
            return call(
                functools.partial(pack_kernel, blocks=blocks, width=cw),
                (1,), [whole((tokens, width))], [whole((blocks, tokens, cw))] * LANES,
                [b16(blocks, tokens, cw)] * LANES, moved=4 * tokens * width, name="pack",
            )(place, x)
        parts = x.reshape(tokens, blocks, LANES, cw).transpose(2, 1, 0, 3)
        at = jnp.stack(slots)
        return [jnp.take(parts, s ^ lane, axis=0)[at] for s in range(LANES)]

    v_out = pack(values)
    v = [v_out[0]] + [swap(v_out[s], s) for s in range(1, LANES)]
    cot_y = swap(cotangent, 2)
    cots = [cotangent, swap(cotangent, 1), cot_y, swap(cot_y, 1)]
    half = rows // 2
    ring = [[out_weight[:half], out_weight[half:]]]
    for _ in range(1, blocks):
        ring.append([shift(part, 1, True) for part in ring[-1]])
    g_out = pack(gating)
    g = [g_out[0]] + [swap(g_out[s], s) for s in range(1, LANES)]

    rate = decay_rate / float(tokens * count)
    starts = [(slots[m] * LANES + lane) * cw for m in range(blocks)]
    per_group = width // groups
    rates = jnp.stack([lax.dynamic_index_in_dim(rate, at // per_group, 0, False) for at in starts])
    res = jnp.stack([lax.dynamic_slice_in_dim(residue, at, cw, 0) for at in starts]).transpose(0, 2, 1)
    skip = jnp.stack([lax.dynamic_slice_in_dim(skip_gain, at, cw, 0) for at in starts])[:, None, :]
    tiled = jnp.tile(rates, (1, subs))
    rate_col, rate_row = tiled[:, :, None], tiled[:, None, :]
    powers = call(
        lambda place, *refs: powers_kernel(*refs, tokens=tokens, modes=modes),
        (blocks,),
        [block((depth, 1)), block((1, depth)), block((modes, cw))],
        [block((depth, tokens))] * 4 + [block((tokens, depth))] * 4 + [block((SUB, cw))],
        [b16(blocks, depth, tokens)] * 4 + [b16(blocks, tokens, depth)] * 4 + [f32(blocks, SUB, cw)],
        moved=blocks * depth * tokens * 16, name="powers",
    )(place, rate_col, rate_row, res)
    af, ab, lf, lb, taps = powers[0:2], powers[2:4], powers[4:6], powers[6:8], powers[8]

    scratch = [
        pltpu.VMEM((tokens, cw), F32),
        pltpu.VMEM((LANES, modes, cw), F32),
        pltpu.VMEM((LANES, modes, cw), F32),
    ]
    common = [block((SUB, cw)), block((modes, cw)), block((depth, 1)), block((1, cw))]
    inner, end = call(
        forward_kernel, (blocks,),
        [block((tokens, cw))] * LANES + [block((depth, tokens))] * 2 + [block((tokens, depth))] * 2 + common,
        [block((span, cw)), block((modes, cw))],
        [f32(blocks, span, cw), f32(blocks, modes, cw)],
        scratch, flops=blocks * 10 * depth * span * cw, moved=blocks * span * cw * 8, name="forward",
    )(place, *v, *af, *lf, taps, res, rate_col, skip)
    coming = [shift(end, hop, False) for hop in range(1, blocks)]

    def at_slot(m):
        return lambda shape: block(shape, m)

    convs, mixeds, wgrads = [None] * blocks, [None] * blocks, [None] * blocks
    for m in list(range(1, blocks)) + [0]:
        here = at_slot(m)
        convs[m], mixeds[m], wgrads[m] = call(
            functools.partial(mixed_kernel, hops=blocks - 1), (1,),
            [block((modes, cw), (m - hop) % blocks) for hop in range(1, blocks)]
            + [here((tokens, cw))] * LANES + [whole((tokens, width))] * LANES
            + [here((span, cw)), here((tokens, depth)), here((tokens, depth)), here((modes, cw)), here((depth, 1))],
            [whole((span, cw)), whole((span, cw)), whole((cw, width))],
            [f32(span, cw), b16(span, cw), f32(cw, width) if m == 0 else b16(cw, width)],
            flops=2 * span * cw * width, moved=2 * span * width, name="mixed",
        )(place, *coming, *g, *cots, inner, *lf, res, rate_col)
    wgrad = wgrads[0]
    for m in range(1, blocks):
        wgrad = wgrad + shift(wgrads[m], -m, True).astype(F32)

    ggrads, inners, ends = [None] * blocks, [None] * blocks, [None] * blocks
    for m in range(blocks):
        here = at_slot(m)
        out = call(
            backward_kernel, (1,),
            [whole((half, width))] * 2 + [here((tokens, cw))] * LANES + [whole((tokens, width))] * LANES
            + [whole((span, cw)), here((depth, tokens)), here((depth, tokens)), here((tokens, depth)), here((tokens, depth))]
            + [here((SUB, cw)), here((modes, cw)), here((depth, 1)), here((1, cw))],
            [whole((tokens, cw))] * LANES + [whole((span, cw)), whole((modes, cw))],
            [b16(tokens, cw)] * LANES + [f32(span, cw), f32(modes, cw)],
            scratch, flops=2 * span * cw * width + 12 * depth * span * cw, moved=2 * span * width, name="backward",
        )(place, *ring[m], *g, *cots, convs[m], *ab, *lb, taps, res, rate_col, skip)
        ggrads[m], inners[m], ends[m] = out[:LANES], out[LANES], out[LANES + 1]
    end = jnp.stack(ends)
    coming = [shift(end, -hop, False) for hop in range(1, blocks)]

    tile = min(512, width)
    cols = lambda r: pl.BlockSpec((r, tile), lambda i, *_: (0, i))
    sums = call(
        functools.partial(output_kernel, blocks=blocks), (width // tile,),
        [whole((span, cw))] * blocks + [cols(half)] * (2 * blocks),
        [cols(tokens)] * LANES,
        [f32(tokens, width)] + [b16(tokens, width)] * (LANES - 1),
        flops=2 * span * blocks * cw * width, moved=4 * width * blocks * cw, name="output",
    )(place, *mixeds, *[w for pair in ring for w in pair])
    output = sums[0]
    for s in range(1, LANES):
        output = output + swap(sums[s], s).astype(F32)

    vgrads = [None] * blocks
    for m in range(blocks):
        here = at_slot(m)
        vgrads[m] = call(
            functools.partial(value_kernel, hops=blocks - 1), (1,),
            [block((modes, cw), (m + hop) % blocks) for hop in range(1, blocks)]
            + [whole((span, cw)), here((tokens, depth)), here((tokens, depth)), here((modes, cw)), here((depth, 1))],
            [whole((tokens, cw))] * LANES, [b16(tokens, cw)] * LANES,
            flops=6 * span * cw * modes, moved=6 * span * cw, name="value",
        )(place, *coming, inners[m], *lb, res, rate_col)

    def back(pieces):
        return [[pieces[m][s] if s == 0 else swap(pieces[m][s], s) for m in range(blocks)] for s in range(LANES)]

    gg, vg = back(ggrads), back(vgrads)
    if cw % 128 == 0:
        value_grad, gate_grad = call(
            functools.partial(unpack_kernel, blocks=blocks, width=cw), (1,),
            [whole((tokens, cw))] * (2 * LANES * blocks), [whole((tokens, width))] * 2,
            [b16(tokens, width)] * 2, moved=8 * tokens * width, name="unpack",
        )(place, *[x for per in vg for x in per], *[x for per in gg for x in per])
    else:

        def joined(pieces):
            full = jnp.stack([jnp.stack(per) for per in pieces])
            at = jnp.stack(slots)
            full = full[lane ^ jnp.arange(LANES)][:, at]
            return full.transpose(2, 1, 0, 3).reshape(tokens, width)

        value_grad, gate_grad = joined(vg), joined(gg)
    return output.astype(BF16), value_grad, gate_grad, wgrad


def solution(mesh):
    rows = P(("parts", "ctx"), None)
    return jax.shard_map(
        per_device,
        mesh=mesh,
        in_specs=(rows, rows, rows, P("parts", None), P("parts", None), P("parts"), rows),
        out_specs=(rows, rows, rows, rows),
        check_vma=False,
    )
```

```python
import functools

import jax
import jax.numpy as jnp
from jax import lax
from jax.experimental import pallas as pl
from jax.experimental.pallas import tpu as pltpu
from jax.sharding import PartitionSpec as P

SUB = 16
LANES = 4
BF16 = jnp.bfloat16
F32 = jnp.float32
VMEM_LIMIT = 32 * 1024 * 1024


def split(a):
    high = a.astype(BF16)
    return high, (a - high.astype(F32)).astype(BF16)


def dot(a, b, dims=((1,), (0,))):
    return lax.dot_general(a, b, (dims, ((), ())), preferred_element_type=F32)


def dot3(a_high, a_low, b):
    b_high, b_low = split(b)
    return dot(a_high, b_high) + dot(a_low, b_high) + dot(a_high, b_low)


def beside(parts):
    return jnp.concatenate(parts, axis=1)


def call(body, grid, in_specs, out_specs, out_shape, scratch=(), flops=0, moved=0, scalars=1, name=None):
    return pl.pallas_call(
        body,
        grid_spec=pltpu.PrefetchScalarGridSpec(
            num_scalar_prefetch=scalars,
            grid=grid,
            in_specs=in_specs,
            out_specs=out_specs,
            scratch_shapes=list(scratch),
        ),
        out_shape=out_shape,
        compiler_params=pltpu.CompilerParams(vmem_limit_bytes=VMEM_LIMIT),
        cost_estimate=pl.CostEstimate(flops=flops, bytes_accessed=moved, transcendentals=0),
        name=name,
    )


def whole(shape):
    return pl.BlockSpec(shape, lambda *_: (0,) * len(shape))


def block(shape, at=None):
    if at is None:
        return pl.BlockSpec((1,) + shape, lambda i, *_: (i,) + (0,) * len(shape))
    return pl.BlockSpec((1,) + shape, lambda *_: (at,) + (0,) * len(shape))


def powers_kernel(rate_col, rate_row, res, af_h, af_l, ab_h, ab_l, lf_h, lf_l, lb_h, lb_l, taps, *, tokens, modes):
    subs = tokens // SUB
    depth = subs * modes
    row = lax.broadcasted_iota(jnp.int32, (depth, tokens), 0) // modes
    tok = lax.broadcasted_iota(jnp.int32, (depth, tokens), 1)

    def power(steps, rate, valid):
        held = jnp.maximum(steps, 0).astype(F32)
        return jnp.where(valid, jnp.exp(-held * rate), 0.0)

    rc = rate_col[0]
    ahead = SUB * (row + 1) - 1 - tok
    af_h[0], af_l[0] = split(power(ahead, rc, ahead >= 0))
    behind = tok - SUB * row
    ab_h[0], ab_l[0] = split(power(behind, rc, behind >= 0))
    col = lax.broadcasted_iota(jnp.int32, (tokens, depth), 1) // modes
    out = lax.broadcasted_iota(jnp.int32, (tokens, depth), 0)
    inside = out % SUB
    rr = rate_row[0]
    carry = col == subs - 1
    steps = jnp.where(carry, out + 1, inside + 1)
    lf_h[0], lf_l[0] = split(power(steps, rr, carry | (out // SUB == col + 1)))
    carry = col == 0
    steps = jnp.where(carry, tokens - out, SUB - inside)
    lb_h[0], lb_l[0] = split(power(steps, rr, carry | (out // SUB == col - 1)))
    lag = lax.broadcasted_iota(jnp.int32, (SUB, modes), 0).astype(F32)
    taps[0] = lax.dot_general(
        jnp.exp(-lag * rr[:, :modes]),
        res[0],
        (((1,), (0,)), ((), ())),
        precision=lax.Precision.HIGHEST,
        preferred_element_type=F32,
    )


def inner_conv(xs, x_scr, e_scr, c_scr, inner, end, a_h, a_l, l_h, l_l, taps, res, rate_col, skip, lane, exact, back):
    tokens, width = xs[0].shape
    modes = res.shape[0]
    subs = tokens // SUB
    order = range(LANES - 1, -1, -1) if back else range(LANES)
    joined = width % 128 == 0
    groups = [list(range(LANES))] if joined else [[s] for s in range(LANES)]
    starts = [None] * LANES
    for group in groups:
        x = beside([xs[s] for s in group]) if len(group) > 1 else xs[group[0]]
        if exact:
            xh = x.astype(BF16)
            st = dot(a_h, xh) + dot(a_l, xh)
        else:
            st = dot3(a_h, a_l, x)
        for at, s in enumerate(group):
            starts[s] = st[:, at * width : (at + 1) * width]
    for s in range(LANES):
        part = starts[s]
        e_scr[s ^ lane] = part[:modes] if back else part[(subs - 1) * modes :]
    fade = jnp.exp(-float(tokens) * rate_col)
    state = jnp.zeros((modes, width), F32)
    for k in order:
        c_scr[k] = state
        state = fade * state + e_scr[k]
    end[...] = state
    weight = jnp.concatenate([res] * subs, axis=0)
    for group in groups:
        pieces = []
        for s in group:
            c = c_scr[s ^ lane]
            if back:
                full = jnp.concatenate([c, starts[s][modes:]], axis=0)
            else:
                full = jnp.concatenate([starts[s][: (subs - 1) * modes], c], axis=0)
            pieces.append(full * weight)
        w = beside(pieces) if len(pieces) > 1 else pieces[0]
        cross = dot3(l_h, l_l, w)
        for at, s in enumerate(group):
            inner[pl.ds(s * tokens, tokens), :] = cross[:, at * width : (at + 1) * width]
    row = lax.broadcasted_iota(jnp.int32, (SUB, width), 0)
    tap = taps + jnp.where(row == 0, skip, 0.0)
    spread = [jnp.broadcast_to(tap[k : k + 1, :], (subs, width)) for k in range(SUB)]
    for s in range(LANES):
        x_scr[...] = xs[s]
        held = [x_scr[pl.ds(t, subs, stride=SUB), :] for t in range(SUB)]
        for t in range(SUB):
            sources = range(t, SUB) if back else range(t + 1)
            total = None
            for u in sources:
                term = spread[abs(t - u)] * held[u]
                total = term if total is None else total + term
            at = pl.ds(s * tokens + t, subs, stride=SUB)
            inner[at, :] = inner[at, :] + total


def entering(coming, rate_col, span):
    total = None
    for hop, state in enumerate(coming):
        term = state if hop == 0 else jnp.exp(-float(span * hop) * rate_col) * state
        total = term if total is None else total + term
    return total


def cross_conv(state, lead_h, lead_l, res, rate_col, lane, tokens, back):
    width = state.shape[1]
    weighted = state * res
    joined = width % 128 == 0
    parts = []
    for s in range(LANES):
        k = s ^ lane
        steps = ((LANES - 1 - k) if back else k).astype(F32) * float(tokens)
        parts.append(jnp.exp(-steps * rate_col) * weighted)
    if joined:
        cross = dot3(lead_h, lead_l, beside(parts))
        return [cross[:, s * width : (s + 1) * width] for s in range(LANES)]
    return [dot3(lead_h, lead_l, p) for p in parts]


def forward_kernel(place, *refs):
    xs = refs[:LANES]
    a_h, a_l, l_h, l_l, taps, res, rate_col, skip, inner, end, x_scr, e_scr, c_scr = refs[LANES:]
    modes = res.shape[1]
    inner_conv(
        [x[0, 0].astype(F32) for x in xs], x_scr, e_scr, c_scr, inner.at[0], end.at[0],
        a_h[0], a_l[0], l_h[0], l_l[0], taps[0], res[0], rate_col[0][:modes], skip[0], place[0], True, False,
    )


def mixed_kernel(place, *refs, hops):
    coming, refs = refs[:hops], refs[hops:]
    gates, refs = refs[:LANES], refs[LANES:]
    inner, l_h, l_l, res, rate_col, conv, mixed, turned = refs
    tokens = gates[0].shape[2]
    modes = res.shape[1]
    rate = rate_col[0][:modes]
    state = entering([c[0] for c in coming], rate, LANES * tokens)
    depth = l_h.shape[2]
    parts = cross_conv(
        state, l_h[0][:, depth - modes :], l_l[0][:, depth - modes :], res[0], rate, place[0], tokens, False
    )
    for s in range(LANES):
        at = pl.ds(s * tokens, tokens)
        value = inner[0, at, :] + parts[s]
        conv[0, at, :] = value
        product = gates[s][0, 0].astype(F32) * value
        mixed[0, at, :] = product.astype(BF16)
        turned[0, :, s * tokens : (s + 1) * tokens] = product.T.astype(BF16)


def weight_kernel(place, turned, *refs):
    cots, outs = refs[:LANES], refs[LANES:]
    right = jnp.concatenate([cot[...] for cot in cots], axis=0)
    for m, out in enumerate(outs):
        out[...] = dot(turned[m], right).astype(out.dtype)


def grad_kernel(place, *refs, blocks):
    weights, cots, grad = refs[:blocks], refs[blocks : blocks + LANES], refs[-1]
    left = jnp.concatenate([cot[...] for cot in cots], axis=0)
    first = pl.program_id(0) == 0
    for m in range(blocks):
        part = dot(left, weights[m][...], ((1,), (1,)))

        @pl.when(first)
        def _():
            grad[m] = part

        @pl.when(jnp.logical_not(first))
        def _():
            grad[m] = grad[m] + part


def backward_kernel(place, *refs):
    gates, refs = refs[:LANES], refs[LANES:]
    grad, conv, a_h, a_l, l_h, l_l, taps, res, rate_col, skip = refs[:10]
    ggrads = refs[10 : 10 + LANES]
    inner, end, x_scr, e_scr, c_scr = refs[10 + LANES :]
    modes = res.shape[1]
    tokens = gates[0].shape[2]
    backs = []
    for s in range(LANES):
        at = pl.ds(s * tokens, tokens)
        g = grad[0, at, :]
        ggrads[s][0] = (g * conv[0, at, :]).astype(BF16)
        backs.append(g * gates[s][0, 0].astype(F32))
    inner_conv(
        backs, x_scr, e_scr, c_scr, inner.at[0], end.at[0],
        a_h[0], a_l[0], l_h[0], l_l[0], taps[0], res[0], rate_col[0][:modes], skip[0], place[0], False, True,
    )


def value_kernel(place, *refs, hops):
    coming, refs = refs[:hops], refs[hops:]
    inner, l_h, l_l, res, rate_col = refs[:5]
    outs = refs[5:]
    tokens = outs[0].shape[1]
    modes = res.shape[1]
    rate = rate_col[0][:modes]
    state = entering([c[0] for c in coming], rate, LANES * tokens)
    parts = cross_conv(state, l_h[0][:, :modes], l_l[0][:, :modes], res[0], rate, place[0], tokens, True)
    for s in range(LANES):
        outs[s][0] = (inner[0, pl.ds(s * tokens, tokens), :] + parts[s]).astype(BF16)


def output_kernel(place, mixed, *refs, blocks):
    weights, (keep, pass_on, send) = refs[:blocks], refs[blocks:]
    tokens = keep.shape[0]
    width = mixed.shape[2]
    if width % 128 == 0:
        left = beside([mixed[m] for m in range(blocks)])
        right = jnp.concatenate([w[...] for w in weights], axis=0)
        total = dot(left, right)
    else:
        total = 0.0
        for m in range(blocks):
            total = total + dot(mixed[m], weights[m][...])
    keep[...] = total[:tokens]
    send[0] = total[tokens : 2 * tokens].astype(BF16)
    pass_on[...] = total[2 * tokens : 3 * tokens]
    send[1] = total[3 * tokens :].astype(BF16)


def pack_kernel(place, *refs, blocks, width):
    lane, turn = place[0], place[1]
    xs, outs = refs[:2], refs[2:]
    for s in range(LANES):
        for m in range(blocks):
            at = lax.rem(turn - m + blocks, blocks) * LANES + (s ^ lane)
            for which in range(2):
                outs[s][which, m] = xs[which][:, pl.ds(pl.multiple_of(at * width, width), width)]


def unpack_kernel(place, *refs, blocks, width):
    lane, turn = place[0], place[1]
    outs = refs[-2:]
    for which in range(2):
        for s in range(LANES):
            piece = refs[which * LANES + s]
            for m in range(blocks):
                at = lax.rem(turn - m + blocks, blocks) * LANES + (s ^ lane)
                outs[which][:, pl.ds(pl.multiple_of(at * width, width), width)] = piece[m]


def per_device(values, gating, out_weight, residue, decay_rate, skip_gain, cotangent):
    tokens, width = values.shape
    groups, modes = decay_rate.shape
    count = lax.axis_size("ctx")
    blocks = count // LANES
    cw = width // count
    span = LANES * tokens
    subs = tokens // SUB
    depth = subs * modes
    hops = blocks - 1
    me = lax.axis_index("ctx")
    lane, turn = lax.rem(me, LANES), me // LANES
    place = jnp.stack([lane, turn]).astype(jnp.int32)
    tile = min(512, width)
    steps = width // tile

    def swap(x, s):
        return lax.ppermute(x, "ctx", [(i, i ^ s) for i in range(count)])

    def shift(x, hop, wrap):
        pairs = []
        for i in range(count):
            to = i + hop * LANES
            if wrap:
                pairs.append((i, to % count))
            elif 0 <= to < count:
                pairs.append((i, to))
        return lax.ppermute(x, "ctx", pairs)

    f32 = lambda *s: jax.ShapeDtypeStruct(s, F32)
    b16 = lambda *s: jax.ShapeDtypeStruct(s, BF16)

    def by_slot(x):
        turned = x[::-1]
        return lax.dynamic_slice_in_dim(jnp.concatenate([turned, turned]), blocks - 1 - turn, blocks, 0)

    def by_lane(pieces):
        one = jnp.bitwise_and(lane, 1) == 1
        two = jnp.bitwise_and(lane, 2) == 2
        pieces = [jnp.where(one, pieces[s ^ 1], pieces[s]) for s in range(LANES)]
        return [jnp.where(two, pieces[s ^ 2], pieces[s]) for s in range(LANES)]

    aligned = cw % 128 == 0
    if aligned:
        sent = call(
            functools.partial(pack_kernel, blocks=blocks, width=cw),
            (1,), [whole((tokens, width))] * 2, [whole((2, blocks, tokens, cw))] * LANES,
            [b16(2, blocks, tokens, cw)] * LANES, moved=8 * tokens * width, name="pack",
        )(place, values, gating)
    else:

        def parts(x):
            return by_slot(x.reshape(tokens, blocks, LANES, cw).transpose(1, 2, 0, 3))

        pv, pg = parts(values), parts(gating)
        sent = by_lane([jnp.stack([pv[:, s], pg[:, s]]) for s in range(LANES)])
    vg = [sent[0]] + [swap(sent[s], s) for s in range(1, LANES)]
    cot_y = swap(cotangent, 2)
    cots = [cotangent, swap(cotangent, 1), cot_y, swap(cot_y, 1)]
    ring = [out_weight]
    for _ in range(hops):
        ring.append(shift(ring[-1], 1, True))

    def own(x):
        x = x.reshape((blocks, LANES) + x.shape[1:])
        return by_slot(lax.dynamic_index_in_dim(x, lane, 1, False))

    rate = decay_rate / float(tokens * count)
    rates = own(jnp.repeat(rate, count // groups, axis=0))
    res = own(residue.reshape(count, cw, modes)).transpose(0, 2, 1)
    skip = own(skip_gain.reshape(count, cw))[:, None, :]
    tiled = jnp.tile(rates, (1, subs))
    rate_col, rate_row = tiled[:, :, None], tiled[:, None, :]
    powers = call(
        lambda place, *refs: powers_kernel(*refs, tokens=tokens, modes=modes),
        (blocks,),
        [block((depth, 1)), block((1, depth)), block((modes, cw))],
        [block((depth, tokens))] * 4 + [block((tokens, depth))] * 4 + [block((SUB, cw))],
        [b16(blocks, depth, tokens)] * 4 + [b16(blocks, tokens, depth)] * 4 + [f32(blocks, SUB, cw)],
        moved=blocks * depth * tokens * 16, name="powers",
    )(place, rate_col, rate_row, res)
    af, ab, lf, lb, taps = powers[0:2], powers[2:4], powers[4:6], powers[6:8], powers[8]

    scratch = [
        pltpu.VMEM((tokens, cw), F32),
        pltpu.VMEM((LANES, modes, cw), F32),
        pltpu.VMEM((LANES, modes, cw), F32),
    ]
    common = [block((SUB, cw)), block((modes, cw)), block((depth, 1)), block((1, cw))]
    lead = [block((tokens, depth))] * 2 + [block((modes, cw)), block((depth, 1))]
    value_part = [pl.BlockSpec((1, 1, tokens, cw), lambda i, *_: (0, i, 0, 0))] * LANES
    gate_part = [pl.BlockSpec((1, 1, tokens, cw), lambda i, *_: (1, i, 0, 0))] * LANES
    cols = lambda r: pl.BlockSpec((r, tile), lambda i, *_: (0, i))

    def state_part(sign):
        return [
            pl.BlockSpec((1, modes, cw), lambda i, *_, h=h: (lax.rem(i + sign * h + blocks, blocks), 0, 0))
            for h in range(1, blocks)
        ]

    inner, end = call(
        forward_kernel, (blocks,),
        value_part + [block((depth, tokens))] * 2 + [block((tokens, depth))] * 2 + common,
        [block((span, cw)), block((modes, cw))],
        [f32(blocks, span, cw), f32(blocks, modes, cw)],
        scratch, flops=blocks * 10 * depth * span * cw, moved=blocks * span * cw * 8, name="forward",
    )(place, *vg, *af, *lf, taps, res, rate_col, skip)
    coming = [shift(end, hop, False) for hop in range(1, blocks)]
    conv, mixed, turned = call(
        functools.partial(mixed_kernel, hops=hops), (blocks,),
        state_part(-1) + gate_part + [block((span, cw))] + lead,
        [block((span, cw)), block((span, cw)), block((cw, span))],
        [f32(blocks, span, cw), b16(blocks, span, cw), b16(blocks, cw, span)],
        flops=blocks * 6 * span * cw * modes, moved=blocks * span * cw * 14, name="mixed",
    )(place, *coming, *vg, inner, *lf, res, rate_col)
    wgrads = call(
        weight_kernel, (steps,),
        [whole((blocks, cw, span))] + [cols(tokens)] * LANES,
        [cols(cw)] * blocks, [f32(cw, width)] + [b16(cw, width)] * hops,
        flops=2 * blocks * span * cw * width, moved=4 * span * width, name="weight",
    )(place, turned, *cots)
    wgrad = wgrads[0]
    for m in range(1, blocks):
        wgrad = wgrad + shift(wgrads[m], -m, True).astype(F32)

    grad = call(
        functools.partial(grad_kernel, blocks=blocks), (steps,),
        [cols(cw)] * blocks + [cols(tokens)] * LANES,
        whole((blocks, span, cw)), f32(blocks, span, cw),
        flops=2 * blocks * span * cw * width, moved=4 * span * width, name="grad",
    )(place, *ring, *cots)
    out = call(
        backward_kernel, (blocks,),
        gate_part + [block((span, cw))] * 2 + [block((depth, tokens))] * 2 + [block((tokens, depth))] * 2 + common,
        [block((tokens, cw))] * LANES + [block((span, cw)), block((modes, cw))],
        [b16(blocks, tokens, cw)] * LANES + [f32(blocks, span, cw), f32(blocks, modes, cw)],
        scratch, flops=blocks * 12 * depth * span * cw, moved=blocks * span * cw * 20, name="backward",
    )(place, *vg, grad, conv, *ab, *lb, taps, res, rate_col, skip)
    ggrads, inner_back, end_back = out[:LANES], out[LANES], out[LANES + 1]
    coming = [shift(end_back, -hop, False) for hop in range(1, blocks)]

    keep, pass_on, send = call(
        functools.partial(output_kernel, blocks=blocks), (steps,),
        [whole((blocks, span, cw))] + [cols(cw)] * blocks,
        [cols(tokens), cols(tokens), pl.BlockSpec((2, tokens, tile), lambda i, *_: (0, 0, i))],
        [f32(tokens, width), f32(tokens, width), b16(2, tokens, width)],
        flops=2 * span * blocks * cw * width, moved=4 * width * blocks * cw, name="output",
    )(place, mixed, *ring)
    near = swap(send, 1)
    far = swap((pass_on + near[1].astype(F32)).astype(BF16), 2)
    output = keep + near[0].astype(F32) + far.astype(F32)

    vgrads = call(
        functools.partial(value_kernel, hops=hops), (blocks,),
        state_part(1) + [block((span, cw))] + lead,
        [block((tokens, cw))] * LANES, [b16(blocks, tokens, cw)] * LANES,
        flops=blocks * 6 * span * cw * modes, moved=blocks * 6 * span * cw, name="value",
    )(place, *coming, inner_back, *lb, res, rate_col)
    gg = [ggrads[0]] + [swap(ggrads[s], s) for s in range(1, LANES)]
    vv = [vgrads[0]] + [swap(vgrads[s], s) for s in range(1, LANES)]
    if aligned:
        value_grad, gate_grad = call(
            functools.partial(unpack_kernel, blocks=blocks, width=cw), (1,),
            [whole((blocks, tokens, cw))] * (2 * LANES), [whole((tokens, width))] * 2,
            [b16(tokens, width)] * 2, moved=8 * tokens * width, name="unpack",
        )(place, *vv, *gg)
    else:

        def joined(pieces):
            full = by_slot(jnp.stack(by_lane(pieces), axis=1))
            return full.transpose(2, 0, 1, 3).reshape(tokens, width)

        value_grad, gate_grad = joined(vv), joined(gg)
    return output.astype(BF16), value_grad, gate_grad, wgrad


def solution(mesh):
    rows = P(("parts", "ctx"), None)
    return jax.shard_map(
        per_device,
        mesh=mesh,
        in_specs=(rows, rows, rows, P("parts", None), P("parts", None), P("parts"), rows),
        out_specs=(rows, rows, rows, rows),
        check_vma=False,
    )
```

```python
import functools

import jax
import jax.numpy as jnp
from jax import lax
from jax.experimental import pallas as pl
from jax.experimental.pallas import tpu as pltpu
from jax.sharding import PartitionSpec as P

SUB = 16
LANES = 4
BF16 = jnp.bfloat16
F32 = jnp.float32
VMEM_LIMIT = 32 * 1024 * 1024


def split(a):
    high = a.astype(BF16)
    return high, (a - high.astype(F32)).astype(BF16)


def dot(a, b, dims=((1,), (0,))):
    return lax.dot_general(a, b, (dims, ((), ())), preferred_element_type=F32)


def dot3(a_high, a_low, b):
    b_high, b_low = split(b)
    return dot(a_high, b_high) + dot(a_low, b_high) + dot(a_high, b_low)


def beside(parts):
    return jnp.concatenate(parts, axis=1)


def call(body, grid, in_specs, out_specs, out_shape, scratch=(), flops=0, moved=0, scalars=1, name=None):
    return pl.pallas_call(
        body,
        grid_spec=pltpu.PrefetchScalarGridSpec(
            num_scalar_prefetch=scalars,
            grid=grid,
            in_specs=in_specs,
            out_specs=out_specs,
            scratch_shapes=list(scratch),
        ),
        out_shape=out_shape,
        compiler_params=pltpu.CompilerParams(vmem_limit_bytes=VMEM_LIMIT),
        cost_estimate=pl.CostEstimate(flops=flops, bytes_accessed=moved, transcendentals=0),
        name=name,
    )


def whole(shape):
    return pl.BlockSpec(shape, lambda *_: (0,) * len(shape))


def block(shape, at=None):
    if at is None:
        return pl.BlockSpec((1,) + shape, lambda i, *_: (i,) + (0,) * len(shape))
    return pl.BlockSpec((1,) + shape, lambda *_: (at,) + (0,) * len(shape))


def powers_kernel(rate_col, rate_row, res, af_h, af_l, ab_h, ab_l, lf_h, lf_l, lb_h, lb_l, taps, *, tokens, modes):
    subs = tokens // SUB
    depth = subs * modes
    row = lax.broadcasted_iota(jnp.int32, (depth, tokens), 0) // modes
    tok = lax.broadcasted_iota(jnp.int32, (depth, tokens), 1)

    def power(steps, rate, valid):
        held = jnp.maximum(steps, 0).astype(F32)
        return jnp.where(valid, jnp.exp(-held * rate), 0.0)

    rc = rate_col[0]
    ahead = SUB * (row + 1) - 1 - tok
    af_h[0], af_l[0] = split(power(ahead, rc, ahead >= 0))
    behind = tok - SUB * row
    ab_h[0], ab_l[0] = split(power(behind, rc, behind >= 0))
    col = lax.broadcasted_iota(jnp.int32, (tokens, depth), 1) // modes
    out = lax.broadcasted_iota(jnp.int32, (tokens, depth), 0)
    inside = out % SUB
    rr = rate_row[0]
    carry = col == subs - 1
    steps = jnp.where(carry, out + 1, inside + 1)
    lf_h[0], lf_l[0] = split(power(steps, rr, carry | (out // SUB == col + 1)))
    carry = col == 0
    steps = jnp.where(carry, tokens - out, SUB - inside)
    lb_h[0], lb_l[0] = split(power(steps, rr, carry | (out // SUB == col - 1)))
    lag = lax.broadcasted_iota(jnp.int32, (SUB, modes), 0).astype(F32)
    taps[0] = lax.dot_general(
        jnp.exp(-lag * rr[:, :modes]),
        res[0],
        (((1,), (0,)), ((), ())),
        precision=lax.Precision.HIGHEST,
        preferred_element_type=F32,
    )


def inner_conv(xs, x_scr, e_scr, c_scr, inner, end, a_h, a_l, l_h, l_l, taps, res, rate_col, skip, lane, exact, back):
    tokens, width = xs[0].shape
    modes = res.shape[0]
    subs = tokens // SUB
    order = range(LANES - 1, -1, -1) if back else range(LANES)
    joined = width % 128 == 0
    groups = [list(range(LANES))] if joined else [[s] for s in range(LANES)]
    starts = [None] * LANES
    for group in groups:
        x = beside([xs[s] for s in group]) if len(group) > 1 else xs[group[0]]
        if exact:
            xh = x.astype(BF16)
            st = dot(a_h, xh) + dot(a_l, xh)
        else:
            st = dot3(a_h, a_l, x)
        for at, s in enumerate(group):
            starts[s] = st[:, at * width : (at + 1) * width]
    for s in range(LANES):
        part = starts[s]
        e_scr[s ^ lane] = part[:modes] if back else part[(subs - 1) * modes :]
    fade = jnp.exp(-float(tokens) * rate_col)
    state = jnp.zeros((modes, width), F32)
    for k in order:
        c_scr[k] = state
        state = fade * state + e_scr[k]
    end[...] = state
    weight = jnp.concatenate([res] * subs, axis=0)
    for group in groups:
        pieces = []
        for s in group:
            c = c_scr[s ^ lane]
            if back:
                full = jnp.concatenate([c, starts[s][modes:]], axis=0)
            else:
                full = jnp.concatenate([starts[s][: (subs - 1) * modes], c], axis=0)
            pieces.append(full * weight)
        w = beside(pieces) if len(pieces) > 1 else pieces[0]
        cross = dot3(l_h, l_l, w)
        for at, s in enumerate(group):
            inner[pl.ds(s * tokens, tokens), :] = cross[:, at * width : (at + 1) * width]
    row = lax.broadcasted_iota(jnp.int32, (SUB, width), 0)
    tap = taps + jnp.where(row == 0, skip, 0.0)
    spread = [jnp.broadcast_to(tap[k : k + 1, :], (subs, width)) for k in range(SUB)]
    for s in range(LANES):
        x_scr[...] = xs[s]
        held = [x_scr[pl.ds(t, subs, stride=SUB), :] for t in range(SUB)]
        for t in range(SUB):
            sources = range(t, SUB) if back else range(t + 1)
            total = None
            for u in sources:
                term = spread[abs(t - u)] * held[u]
                total = term if total is None else total + term
            at = pl.ds(s * tokens + t, subs, stride=SUB)
            inner[at, :] = inner[at, :] + total


def cross_conv(state, lead_h, lead_l, res, rate_col, lane, tokens, back):
    width = state.shape[1]
    weighted = state * res
    joined = width % 128 == 0
    parts = []
    for s in range(LANES):
        k = s ^ lane
        steps = ((LANES - 1 - k) if back else k).astype(F32) * float(tokens)
        parts.append(jnp.exp(-steps * rate_col) * weighted)
    if joined:
        cross = dot3(lead_h, lead_l, beside(parts))
        return [cross[:, s * width : (s + 1) * width] for s in range(LANES)]
    return [dot3(lead_h, lead_l, p) for p in parts]


def forward_kernel(place, *refs):
    xs = refs[:LANES]
    a_h, a_l, l_h, l_l, taps, res, rate_col, skip, inner, end, x_scr, e_scr, c_scr = refs[LANES:]
    modes = res.shape[1]
    inner_conv(
        [x[0, 0].astype(F32) for x in xs], x_scr, e_scr, c_scr, inner.at[0], end.at[0],
        a_h[0], a_l[0], l_h[0], l_l[0], taps[0], res[0], rate_col[0][:modes], skip[0], place[0], True, False,
    )


def mixed_kernel(place, coming, *refs):
    gates, refs = refs[:LANES], refs[LANES:]
    inner, l_h, l_l, res, rate_col, conv, mixed, turned = refs
    tokens = gates[0].shape[2]
    modes = res.shape[1]
    rate = rate_col[0][:modes]
    state = coming[0]
    depth = l_h.shape[2]
    parts = cross_conv(
        state, l_h[0][:, depth - modes :], l_l[0][:, depth - modes :], res[0], rate, place[0], tokens, False
    )
    for s in range(LANES):
        at = pl.ds(s * tokens, tokens)
        value = inner[0, at, :] + parts[s]
        conv[0, at, :] = value
        product = gates[s][0, 0].astype(F32) * value
        mixed[0, at, :] = product.astype(BF16)
        turned[0, :, s * tokens : (s + 1) * tokens] = product.T.astype(BF16)


def weight_kernel(place, turned, *refs):
    cots, outs = refs[:LANES], refs[LANES:]
    right = jnp.concatenate([cot[...] for cot in cots], axis=0)
    for m, out in enumerate(outs):
        out[...] = dot(turned[m], right).astype(out.dtype)


def grad_kernel(place, *refs, blocks):
    weights, cots, grad = refs[:blocks], refs[blocks : blocks + LANES], refs[-1]
    left = jnp.concatenate([cot[...] for cot in cots], axis=0)
    width = weights[0].shape[0]
    first = pl.program_id(0) == 0
    if width % 128 == 0:
        right = jnp.concatenate([w[...] for w in weights], axis=0)
        wide = dot(left, right, ((1,), (1,)))
        parts = [wide[:, m * width : (m + 1) * width] for m in range(blocks)]
    else:
        parts = [dot(left, w[...], ((1,), (1,))) for w in weights]

    @pl.when(first)
    def _():
        for m in range(blocks):
            grad[m] = parts[m]

    @pl.when(jnp.logical_not(first))
    def _():
        for m in range(blocks):
            grad[m] = grad[m] + parts[m]


def backward_kernel(place, *refs):
    gates, refs = refs[:LANES], refs[LANES:]
    grad, conv, a_h, a_l, l_h, l_l, taps, res, rate_col, skip = refs[:10]
    ggrads = refs[10 : 10 + LANES]
    inner, end, x_scr, e_scr, c_scr = refs[10 + LANES :]
    modes = res.shape[1]
    tokens = gates[0].shape[2]
    backs = []
    for s in range(LANES):
        at = pl.ds(s * tokens, tokens)
        g = grad[0, at, :]
        ggrads[s][0] = (g * conv[0, at, :]).astype(BF16)
        backs.append(g * gates[s][0, 0].astype(F32))
    inner_conv(
        backs, x_scr, e_scr, c_scr, inner.at[0], end.at[0],
        a_h[0], a_l[0], l_h[0], l_l[0], taps[0], res[0], rate_col[0][:modes], skip[0], place[0], False, True,
    )


def value_kernel(place, coming, *refs):
    inner, l_h, l_l, res, rate_col = refs[:5]
    outs = refs[5:]
    tokens = outs[0].shape[1]
    modes = res.shape[1]
    rate = rate_col[0][:modes]
    state = coming[0]
    parts = cross_conv(state, l_h[0][:, :modes], l_l[0][:, :modes], res[0], rate, place[0], tokens, True)
    for s in range(LANES):
        outs[s][0] = (inner[0, pl.ds(s * tokens, tokens), :] + parts[s]).astype(BF16)


def output_kernel(place, mixed, *refs, blocks):
    weights, (keep, pass_on, send) = refs[:blocks], refs[blocks:]
    tokens = keep.shape[0]
    width = mixed.shape[2]
    if width % 128 == 0:
        left = beside([mixed[m] for m in range(blocks)])
        right = jnp.concatenate([w[...] for w in weights], axis=0)
        total = dot(left, right)
    else:
        total = 0.0
        for m in range(blocks):
            total = total + dot(mixed[m], weights[m][...])
    keep[...] = total[:tokens]
    send[0] = total[tokens : 2 * tokens].astype(BF16)
    pass_on[...] = total[2 * tokens : 3 * tokens]
    send[1] = total[3 * tokens :].astype(BF16)


def pack_kernel(place, *refs, blocks, width):
    lane, turn = place[0], place[1]
    xs, outs = refs[:2], refs[2:]
    for s in range(LANES):
        for m in range(blocks):
            at = lax.rem(turn - m + blocks, blocks) * LANES + (s ^ lane)
            for which in range(2):
                outs[s][which, m] = xs[which][:, pl.ds(pl.multiple_of(at * width, width), width)]


def unpack_kernel(place, *refs, blocks, width):
    lane, turn = place[0], place[1]
    outs = refs[-2:]
    for which in range(2):
        for s in range(LANES):
            piece = refs[which * LANES + s]
            for m in range(blocks):
                at = lax.rem(turn - m + blocks, blocks) * LANES + (s ^ lane)
                outs[which][:, pl.ds(pl.multiple_of(at * width, width), width)] = piece[m]


def per_device(values, gating, out_weight, residue, decay_rate, skip_gain, cotangent):
    tokens, width = values.shape
    groups, modes = decay_rate.shape
    count = lax.axis_size("ctx")
    blocks = count // LANES
    cw = width // count
    span = LANES * tokens
    subs = tokens // SUB
    depth = subs * modes
    hops = blocks - 1
    me = lax.axis_index("ctx")
    lane, turn = lax.rem(me, LANES), me // LANES
    place = jnp.stack([lane, turn]).astype(jnp.int32)
    tile = min(512, width)
    steps = width // tile

    def swap(x, s):
        return lax.ppermute(x, "ctx", [(i, i ^ s) for i in range(count)])

    def shift(x, hop, wrap):
        pairs = []
        for i in range(count):
            to = i + hop * LANES
            if wrap:
                pairs.append((i, to % count))
            elif 0 <= to < count:
                pairs.append((i, to))
        return lax.ppermute(x, "ctx", pairs)

    def after(x, *others):
        return lax.optimization_barrier((x,) + others)[0]

    f32 = lambda *s: jax.ShapeDtypeStruct(s, F32)
    b16 = lambda *s: jax.ShapeDtypeStruct(s, BF16)

    def by_slot(x):
        turned = x[::-1]
        return lax.dynamic_slice_in_dim(jnp.concatenate([turned, turned]), blocks - 1 - turn, blocks, 0)

    def by_lane(pieces):
        one = jnp.bitwise_and(lane, 1) == 1
        two = jnp.bitwise_and(lane, 2) == 2
        pieces = [jnp.where(one, pieces[s ^ 1], pieces[s]) for s in range(LANES)]
        return [jnp.where(two, pieces[s ^ 2], pieces[s]) for s in range(LANES)]

    aligned = cw % 128 == 0
    if aligned:
        sent = call(
            functools.partial(pack_kernel, blocks=blocks, width=cw),
            (1,), [whole((tokens, width))] * 2, [whole((2, blocks, tokens, cw))] * LANES,
            [b16(2, blocks, tokens, cw)] * LANES, moved=8 * tokens * width, name="pack",
        )(place, values, gating)
    else:

        def parts(x):
            return by_slot(x.reshape(tokens, blocks, LANES, cw).transpose(1, 2, 0, 3))

        pv, pg = parts(values), parts(gating)
        sent = by_lane([jnp.stack([pv[:, s], pg[:, s]]) for s in range(LANES)])
    ring = [out_weight, shift(out_weight, 1, True)]
    vg = [sent[0]] + [swap(sent[s], s) for s in (2, 3, 1)]
    vg = [vg[0], vg[3], vg[1], vg[2]]
    cot_y = swap(after(cotangent, *vg[1:]), 2)
    ring.append(shift(after(ring[-1], *vg[1:]), 1, True))

    def own(x):
        x = x.reshape((blocks, LANES) + x.shape[1:])
        return by_slot(lax.dynamic_index_in_dim(x, lane, 1, False))

    rate = decay_rate / float(tokens * count)
    rates = own(jnp.repeat(rate, count // groups, axis=0))
    res = own(residue.reshape(count, cw, modes)).transpose(0, 2, 1)
    skip = own(skip_gain.reshape(count, cw))[:, None, :]
    tiled = jnp.tile(rates, (1, subs))
    rate_col, rate_row = tiled[:, :, None], tiled[:, None, :]
    powers = call(
        lambda place, *refs: powers_kernel(*refs, tokens=tokens, modes=modes),
        (blocks,),
        [block((depth, 1)), block((1, depth)), block((modes, cw))],
        [block((depth, tokens))] * 4 + [block((tokens, depth))] * 4 + [block((SUB, cw))],
        [b16(blocks, depth, tokens)] * 4 + [b16(blocks, tokens, depth)] * 4 + [f32(blocks, SUB, cw)],
        moved=blocks * depth * tokens * 16, name="powers",
    )(place, rate_col, rate_row, res)
    af, ab, lf, lb, taps = powers[0:2], powers[2:4], powers[4:6], powers[6:8], powers[8]

    scratch = [
        pltpu.VMEM((tokens, cw), F32),
        pltpu.VMEM((LANES, modes, cw), F32),
        pltpu.VMEM((LANES, modes, cw), F32),
    ]
    common = [block((SUB, cw)), block((modes, cw)), block((depth, 1)), block((1, cw))]
    lead = [block((tokens, depth))] * 2 + [block((modes, cw)), block((depth, 1))]
    value_part = [pl.BlockSpec((1, 1, tokens, cw), lambda i, *_: (0, i, 0, 0))] * LANES
    gate_part = [pl.BlockSpec((1, 1, tokens, cw), lambda i, *_: (1, i, 0, 0))] * LANES
    cols = lambda r: pl.BlockSpec((r, tile), lambda i, *_: (0, i))

    def scan(own_end, sign):
        fade = jnp.exp(-float(span) * rates)[:, :, None]
        total, held, hop, first = None, own_end, 1, None
        while hop < blocks:
            got = jnp.roll(shift(held.astype(BF16), sign * hop, False), sign * hop, axis=0).astype(F32)
            first = got if first is None else first
            total = got if total is None else total + fade ** (hop - 1) * got
            held = held + fade**hop * got
            hop *= 2
        return total, first

    inner, end = call(
        forward_kernel, (blocks,),
        value_part + [block((depth, tokens))] * 2 + [block((tokens, depth))] * 2 + common,
        [block((span, cw)), block((modes, cw))],
        [f32(blocks, span, cw), f32(blocks, modes, cw)],
        scratch, flops=blocks * 10 * depth * span * cw, moved=blocks * span * cw * 8, name="forward",
    )(place, *vg, *af, *lf, taps, res, rate_col, skip)
    cots = [cotangent, swap(after(cotangent, end), 1), cot_y, swap(after(cot_y, end), 1)]
    coming, first = scan(end, 1)
    ring.append(shift(after(ring[-1], first), 1, True))
    for _ in range(blocks - len(ring)):
        ring.append(shift(ring[-1], 1, True))
    conv, mixed, turned = call(
        mixed_kernel, (blocks,),
        [block((modes, cw))] + gate_part + [block((span, cw))] + lead,
        [block((span, cw)), block((span, cw)), block((cw, span))],
        [f32(blocks, span, cw), b16(blocks, span, cw), b16(blocks, cw, span)],
        flops=blocks * 6 * span * cw * modes, moved=blocks * span * cw * 14, name="mixed",
    )(place, coming, *vg, inner, *lf, res, rate_col)
    wgrads = call(
        weight_kernel, (steps,),
        [whole((blocks, cw, span))] + [cols(tokens)] * LANES,
        [cols(cw)] * blocks, [f32(cw, width)] * hops + [b16(cw, width)],
        flops=2 * blocks * span * cw * width, moved=4 * span * width, name="weight",
    )(place, turned, *cots)
    part = shift(wgrads[-1], -1, True)

    def pass_on_sum(part, m):
        return shift((wgrads[m] + part.astype(F32)).astype(BF16), -1, True)

    grad = call(
        functools.partial(grad_kernel, blocks=blocks), (steps,),
        [cols(cw)] * blocks + [cols(tokens)] * LANES,
        whole((blocks, span, cw)), f32(blocks, span, cw),
        flops=2 * blocks * span * cw * width, moved=4 * span * width, name="grad",
    )(place, *ring, *after(tuple(cots), wgrads))
    out = call(
        backward_kernel, (blocks,),
        gate_part + [block((span, cw))] * 2 + [block((depth, tokens))] * 2 + [block((tokens, depth))] * 2 + common,
        [block((tokens, cw))] * LANES + [block((span, cw)), block((modes, cw))],
        [b16(blocks, tokens, cw)] * LANES + [f32(blocks, span, cw), f32(blocks, modes, cw)],
        scratch, flops=blocks * 12 * depth * span * cw, moved=blocks * span * cw * 20, name="backward",
    )(place, *vg, grad, conv, *ab, *lb, taps, res, rate_col, skip)
    ggrads, inner_back, end_back = out[:LANES], out[LANES], out[LANES + 1]
    coming, first = scan(end_back, -1)
    part = pass_on_sum(after(part, end_back), blocks - 2)

    keep, pass_on, send = call(
        functools.partial(output_kernel, blocks=blocks), (steps,),
        [whole((blocks, span, cw))] + [cols(cw)] * blocks,
        [cols(tokens), cols(tokens), pl.BlockSpec((2, tokens, tile), lambda i, *_: (0, 0, i))],
        [f32(tokens, width), f32(tokens, width), b16(2, tokens, width)],
        flops=2 * span * blocks * cw * width, moved=4 * width * blocks * cw, name="output",
    )(place, after(mixed, end_back), *ring)
    near = swap(send, 1)
    far = swap((pass_on + near[1].astype(F32)).astype(BF16), 2)
    output = keep + near[0].astype(F32) + far.astype(F32)

    vgrads = call(
        value_kernel, (blocks,),
        [block((modes, cw))] + [block((span, cw))] + lead,
        [block((tokens, cw))] * LANES, [b16(blocks, tokens, cw)] * LANES,
        flops=blocks * 6 * span * cw * modes, moved=blocks * 6 * span * cw, name="value",
    )(place, coming, inner_back, *lb, res, rate_col)
    for m in range(blocks - 3, 0, -1):
        part = pass_on_sum(after(part, coming) if m == blocks - 3 else part, m)
    wgrad = wgrads[0] + part.astype(F32)
    gg = [ggrads[0]] + [swap(after(ggrads[s], far), s) for s in range(1, LANES)]
    vv = [vgrads[0]] + [swap(vgrads[s], s) for s in range(1, LANES)]
    if aligned:
        value_grad, gate_grad = call(
            functools.partial(unpack_kernel, blocks=blocks, width=cw), (1,),
            [whole((blocks, tokens, cw))] * (2 * LANES), [whole((tokens, width))] * 2,
            [b16(tokens, width)] * 2, moved=8 * tokens * width, name="unpack",
        )(place, *vv, *gg)
    else:

        def joined(pieces):
            full = by_slot(jnp.stack(by_lane(pieces), axis=1))
            return full.transpose(2, 0, 1, 3).reshape(tokens, width)

        value_grad, gate_grad = joined(vv), joined(gg)
    return output.astype(BF16), value_grad, gate_grad, wgrad


def solution(mesh):
    rows = P(("parts", "ctx"), None)
    return jax.shard_map(
        per_device,
        mesh=mesh,
        in_specs=(rows, rows, rows, P("parts", None), P("parts", None), P("parts"), rows),
        out_specs=(rows, rows, rows, rows),
        check_vma=False,
    )
```

```python
import functools

import jax
import jax.numpy as jnp
from jax import lax
from jax.experimental import pallas as pl
from jax.experimental.pallas import tpu as pltpu
from jax.sharding import PartitionSpec as P

SUB = 16
LANES = 4
BF16 = jnp.bfloat16
F32 = jnp.float32
VMEM_LIMIT = 32 * 1024 * 1024


def split(a):
    high = a.astype(BF16)
    return high, (a - high.astype(F32)).astype(BF16)


def dot(a, b, dims=((1,), (0,))):
    return lax.dot_general(a, b, (dims, ((), ())), preferred_element_type=F32)


def dot3(a_high, a_low, b):
    b_high, b_low = split(b)
    return dot(a_high, b_high) + dot(a_low, b_high) + dot(a_high, b_low)


def beside(parts):
    return jnp.concatenate(parts, axis=1)


def call(body, grid, in_specs, out_specs, out_shape, scratch=(), flops=0, moved=0, scalars=1, name=None):
    return pl.pallas_call(
        body,
        grid_spec=pltpu.PrefetchScalarGridSpec(
            num_scalar_prefetch=scalars,
            grid=grid,
            in_specs=in_specs,
            out_specs=out_specs,
            scratch_shapes=list(scratch),
        ),
        out_shape=out_shape,
        compiler_params=pltpu.CompilerParams(vmem_limit_bytes=VMEM_LIMIT),
        cost_estimate=pl.CostEstimate(flops=flops, bytes_accessed=moved, transcendentals=0),
        name=name,
    )


def whole(shape):
    return pl.BlockSpec(shape, lambda *_: (0,) * len(shape))


def block(shape, at=None):
    if at is None:
        return pl.BlockSpec((1,) + shape, lambda i, *_: (i,) + (0,) * len(shape))
    return pl.BlockSpec((1,) + shape, lambda *_: (at,) + (0,) * len(shape))


def powers_kernel(rate_col, rate_row, res, af_h, af_l, ab_h, ab_l, lf_h, lf_l, lb_h, lb_l, taps, *, tokens, modes):
    subs = tokens // SUB
    depth = subs * modes
    row = lax.broadcasted_iota(jnp.int32, (depth, tokens), 0) // modes
    tok = lax.broadcasted_iota(jnp.int32, (depth, tokens), 1)

    def power(steps, rate, valid):
        held = jnp.maximum(steps, 0).astype(F32)
        return jnp.where(valid, jnp.exp(-held * rate), 0.0)

    rc = rate_col[0]
    ahead = SUB * (row + 1) - 1 - tok
    af_h[0], af_l[0] = split(power(ahead, rc, ahead >= 0))
    behind = tok - SUB * row
    ab_h[0], ab_l[0] = split(power(behind, rc, behind >= 0))
    col = lax.broadcasted_iota(jnp.int32, (tokens, depth), 1) // modes
    out = lax.broadcasted_iota(jnp.int32, (tokens, depth), 0)
    inside = out % SUB
    rr = rate_row[0]
    carry = col == subs - 1
    steps = jnp.where(carry, out + 1, inside + 1)
    lf_h[0], lf_l[0] = split(power(steps, rr, carry | (out // SUB == col + 1)))
    carry = col == 0
    steps = jnp.where(carry, tokens - out, SUB - inside)
    lb_h[0], lb_l[0] = split(power(steps, rr, carry | (out // SUB == col - 1)))
    lag = lax.broadcasted_iota(jnp.int32, (SUB, modes), 0).astype(F32)
    taps[0] = lax.dot_general(
        jnp.exp(-lag * rr[:, :modes]),
        res[0],
        (((1,), (0,)), ((), ())),
        precision=lax.Precision.HIGHEST,
        preferred_element_type=F32,
    )


def inner_conv(xs, x_scr, e_scr, c_scr, inner, end, a_h, a_l, l_h, l_l, taps, res, rate_col, skip, lane, exact, back):
    tokens, width = xs[0].shape
    modes = res.shape[0]
    subs = tokens // SUB
    order = range(LANES - 1, -1, -1) if back else range(LANES)
    joined = width % 128 == 0
    groups = [list(range(LANES))] if joined else [[s] for s in range(LANES)]
    starts = [None] * LANES
    for group in groups:
        x = beside([xs[s] for s in group]) if len(group) > 1 else xs[group[0]]
        if exact:
            xh = x.astype(BF16)
            st = dot(a_h, xh) + dot(a_l, xh)
        else:
            st = dot3(a_h, a_l, x)
        for at, s in enumerate(group):
            starts[s] = st[:, at * width : (at + 1) * width]
    for s in range(LANES):
        part = starts[s]
        e_scr[s ^ lane] = part[:modes] if back else part[(subs - 1) * modes :]
    fade = jnp.exp(-float(tokens) * rate_col)
    state = jnp.zeros((modes, width), F32)
    for k in order:
        c_scr[k] = state
        state = fade * state + e_scr[k]
    end[...] = state
    weight = jnp.concatenate([res] * subs, axis=0)
    for group in groups:
        pieces = []
        for s in group:
            c = c_scr[s ^ lane]
            if back:
                full = jnp.concatenate([c, starts[s][modes:]], axis=0)
            else:
                full = jnp.concatenate([starts[s][: (subs - 1) * modes], c], axis=0)
            pieces.append(full * weight)
        w = beside(pieces) if len(pieces) > 1 else pieces[0]
        cross = dot3(l_h, l_l, w)
        for at, s in enumerate(group):
            inner[pl.ds(s * tokens, tokens), :] = cross[:, at * width : (at + 1) * width]
    row = lax.broadcasted_iota(jnp.int32, (SUB, width), 0)
    tap = taps + jnp.where(row == 0, skip, 0.0)
    spread = [jnp.broadcast_to(tap[k : k + 1, :], (subs, width)) for k in range(SUB)]
    for s in range(LANES):
        x_scr[...] = xs[s]
        held = [x_scr[pl.ds(t, subs, stride=SUB), :] for t in range(SUB)]
        for t in range(SUB):
            sources = range(t, SUB) if back else range(t + 1)
            total = None
            for u in sources:
                term = spread[abs(t - u)] * held[u]
                total = term if total is None else total + term
            at = pl.ds(s * tokens + t, subs, stride=SUB)
            inner[at, :] = inner[at, :] + total


def cross_conv(state, lead_h, lead_l, res, rate_col, lane, tokens, back):
    width = state.shape[1]
    weighted = state * res
    joined = width % 128 == 0
    parts = []
    for s in range(LANES):
        k = s ^ lane
        steps = ((LANES - 1 - k) if back else k).astype(F32) * float(tokens)
        parts.append(jnp.exp(-steps * rate_col) * weighted)
    if joined:
        cross = dot3(lead_h, lead_l, beside(parts))
        return [cross[:, s * width : (s + 1) * width] for s in range(LANES)]
    return [dot3(lead_h, lead_l, p) for p in parts]


def forward_kernel(place, *refs):
    xs = refs[:LANES]
    a_h, a_l, l_h, l_l, taps, res, rate_col, skip, inner, end, x_scr, e_scr, c_scr = refs[LANES:]
    modes = res.shape[1]
    inner_conv(
        [x[0, 0].astype(F32) for x in xs], x_scr, e_scr, c_scr, inner.at[0], end.at[0],
        a_h[0], a_l[0], l_h[0], l_l[0], taps[0], res[0], rate_col[0][:modes], skip[0], place[0], True, False,
    )


def mixed_kernel(place, coming, *refs):
    gates, refs = refs[:LANES], refs[LANES:]
    inner, l_h, l_l, res, rate_col, conv, mixed, turned = refs
    tokens = gates[0].shape[2]
    modes = res.shape[1]
    rate = rate_col[0][:modes]
    state = coming[0]
    depth = l_h.shape[2]
    parts = cross_conv(
        state, l_h[0][:, depth - modes :], l_l[0][:, depth - modes :], res[0], rate, place[0], tokens, False
    )
    for s in range(LANES):
        at = pl.ds(s * tokens, tokens)
        value = inner[0, at, :] + parts[s]
        conv[0, at, :] = value
        product = gates[s][0, 0].astype(F32) * value
        mixed[0, at, :] = product.astype(BF16)
        turned[0, :, s * tokens : (s + 1) * tokens] = product.T.astype(BF16)


def weight_kernel(place, turned, *refs):
    cots, outs = refs[:LANES], refs[LANES:]
    right = jnp.concatenate([cot[...] for cot in cots], axis=0)
    for m, out in enumerate(outs):
        out[...] = dot(turned[m], right).astype(out.dtype)


def grad_kernel(place, *refs, blocks):
    weights, cots, grad = refs[:blocks], refs[blocks : blocks + LANES], refs[-1]
    left = jnp.concatenate([cot[...] for cot in cots], axis=0)
    width = weights[0].shape[0]
    first = pl.program_id(0) == 0
    if width % 128 == 0:
        right = jnp.concatenate([w[...] for w in weights], axis=0)
        wide = dot(left, right, ((1,), (1,)))
        parts = [wide[:, m * width : (m + 1) * width] for m in range(blocks)]
    else:
        parts = [dot(left, w[...], ((1,), (1,))) for w in weights]

    @pl.when(first)
    def _():
        for m in range(blocks):
            grad[m] = parts[m]

    @pl.when(jnp.logical_not(first))
    def _():
        for m in range(blocks):
            grad[m] = grad[m] + parts[m]


def backward_kernel(place, *refs):
    gates, refs = refs[:LANES], refs[LANES:]
    grad, conv, a_h, a_l, l_h, l_l, taps, res, rate_col, skip = refs[:10]
    ggrads = refs[10 : 10 + LANES]
    inner, end, x_scr, e_scr, c_scr = refs[10 + LANES :]
    modes = res.shape[1]
    tokens = gates[0].shape[2]
    backs = []
    for s in range(LANES):
        at = pl.ds(s * tokens, tokens)
        g = grad[0, at, :]
        ggrads[s][0] = (g * conv[0, at, :]).astype(BF16)
        backs.append(g * gates[s][0, 0].astype(F32))
    inner_conv(
        backs, x_scr, e_scr, c_scr, inner.at[0], end.at[0],
        a_h[0], a_l[0], l_h[0], l_l[0], taps[0], res[0], rate_col[0][:modes], skip[0], place[0], False, True,
    )


def value_kernel(place, coming, *refs):
    inner, l_h, l_l, res, rate_col = refs[:5]
    outs = refs[5:]
    tokens = outs[0].shape[1]
    modes = res.shape[1]
    rate = rate_col[0][:modes]
    state = coming[0]
    parts = cross_conv(state, l_h[0][:, :modes], l_l[0][:, :modes], res[0], rate, place[0], tokens, True)
    for s in range(LANES):
        outs[s][0] = (inner[0, pl.ds(s * tokens, tokens), :] + parts[s]).astype(BF16)


def output_kernel(place, mixed, *refs, blocks):
    weights, (keep, pass_on, send) = refs[:blocks], refs[blocks:]
    tokens = keep.shape[0]
    width = mixed.shape[2]
    if width % 128 == 0:
        left = beside([mixed[m] for m in range(blocks)])
        right = jnp.concatenate([w[...] for w in weights], axis=0)
        total = dot(left, right)
    else:
        total = 0.0
        for m in range(blocks):
            total = total + dot(mixed[m], weights[m][...])
    keep[...] = total[:tokens]
    send[0] = total[tokens : 2 * tokens].astype(BF16)
    pass_on[...] = total[2 * tokens : 3 * tokens]
    send[1] = total[3 * tokens :].astype(BF16)


def pack_kernel(place, *refs, blocks, width):
    lane, turn = place[0], place[1]
    xs, outs = refs[:2], refs[2:]
    for s in range(LANES):
        for m in range(blocks):
            at = lax.rem(turn - m + blocks, blocks) * LANES + (s ^ lane)
            for which in range(2):
                outs[s][which, m] = xs[which][:, pl.ds(pl.multiple_of(at * width, width), width)]


def unpack_kernel(place, *refs, blocks, width):
    lane, turn = place[0], place[1]
    outs = refs[-2:]
    for which in range(2):
        for s in range(LANES):
            piece = refs[which * LANES + s]
            for m in range(blocks):
                at = lax.rem(turn - m + blocks, blocks) * LANES + (s ^ lane)
                outs[which][:, pl.ds(pl.multiple_of(at * width, width), width)] = piece[m]


def per_device(values, gating, out_weight, residue, decay_rate, skip_gain, cotangent):
    tokens, width = values.shape
    groups, modes = decay_rate.shape
    count = lax.axis_size("ctx")
    blocks = count // LANES
    cw = width // count
    span = LANES * tokens
    subs = tokens // SUB
    depth = subs * modes
    hops = blocks - 1
    me = lax.axis_index("ctx")
    lane, turn = lax.rem(me, LANES), me // LANES
    place = jnp.stack([lane, turn]).astype(jnp.int32)
    tile = min(512, width)
    steps = width // tile

    def swap(x, s):
        return lax.ppermute(x, "ctx", [(i, i ^ s) for i in range(count)])

    def shift(x, hop, wrap):
        pairs = []
        for i in range(count):
            to = i + hop * LANES
            if wrap:
                pairs.append((i, to % count))
            elif 0 <= to < count:
                pairs.append((i, to))
        return lax.ppermute(x, "ctx", pairs)

    def after(x, *others):
        return lax.optimization_barrier((x,) + others)[0]

    f32 = lambda *s: jax.ShapeDtypeStruct(s, F32)
    b16 = lambda *s: jax.ShapeDtypeStruct(s, BF16)

    def by_slot(x):
        turned = x[::-1]
        return lax.dynamic_slice_in_dim(jnp.concatenate([turned, turned]), blocks - 1 - turn, blocks, 0)

    def by_lane(pieces):
        one = jnp.bitwise_and(lane, 1) == 1
        two = jnp.bitwise_and(lane, 2) == 2
        pieces = [jnp.where(one, pieces[s ^ 1], pieces[s]) for s in range(LANES)]
        return [jnp.where(two, pieces[s ^ 2], pieces[s]) for s in range(LANES)]

    aligned = cw % 128 == 0
    if aligned:
        sent = call(
            functools.partial(pack_kernel, blocks=blocks, width=cw),
            (1,), [whole((tokens, width))] * 2, [whole((2, blocks, tokens, cw))] * LANES,
            [b16(2, blocks, tokens, cw)] * LANES, moved=8 * tokens * width, name="pack",
        )(place, values, gating)
    else:

        def parts(x):
            return by_slot(x.reshape(tokens, blocks, LANES, cw).transpose(1, 2, 0, 3))

        pv, pg = parts(values), parts(gating)
        sent = by_lane([jnp.stack([pv[:, s], pg[:, s]]) for s in range(LANES)])
    def own(x):
        x = x.reshape((blocks, LANES) + x.shape[1:])
        return by_slot(lax.dynamic_index_in_dim(x, lane, 1, False))

    rate = decay_rate / float(tokens * count)
    rates = own(jnp.repeat(rate, count // groups, axis=0))
    res = own(residue.reshape(count, cw, modes)).transpose(0, 2, 1)
    skip = own(skip_gain.reshape(count, cw))[:, None, :]
    tiled = jnp.tile(rates, (1, subs))
    rate_col, rate_row = tiled[:, :, None], tiled[:, None, :]
    powers = call(
        lambda place, *refs: powers_kernel(*refs, tokens=tokens, modes=modes),
        (blocks,),
        [block((depth, 1)), block((1, depth)), block((modes, cw))],
        [block((depth, tokens))] * 4 + [block((tokens, depth))] * 4 + [block((SUB, cw))],
        [b16(blocks, depth, tokens)] * 4 + [b16(blocks, tokens, depth)] * 4 + [f32(blocks, SUB, cw)],
        moved=blocks * depth * tokens * 16, name="powers",
    )(place, rate_col, rate_row, res)
    af, ab, lf, lb, taps = powers[0:2], powers[2:4], powers[4:6], powers[6:8], powers[8]

    ring = [out_weight, shift(out_weight, 1, True)]
    vg = [sent[0]] + [swap(sent[s], s) for s in (2, 3, 1)]
    vg = [vg[0], vg[3], vg[1], vg[2]]
    cot_y = swap(after(cotangent, taps, *vg[1:]), 2)
    ring.append(shift(after(ring[-1], taps, *vg[1:]), 1, True))

    scratch = [
        pltpu.VMEM((tokens, cw), F32),
        pltpu.VMEM((LANES, modes, cw), F32),
        pltpu.VMEM((LANES, modes, cw), F32),
    ]
    common = [block((SUB, cw)), block((modes, cw)), block((depth, 1)), block((1, cw))]
    lead = [block((tokens, depth))] * 2 + [block((modes, cw)), block((depth, 1))]
    value_part = [pl.BlockSpec((1, 1, tokens, cw), lambda i, *_: (0, i, 0, 0))] * LANES
    gate_part = [pl.BlockSpec((1, 1, tokens, cw), lambda i, *_: (1, i, 0, 0))] * LANES
    cols = lambda r: pl.BlockSpec((r, tile), lambda i, *_: (0, i))

    def scan(own_end, sign):
        fade = jnp.exp(-float(span) * rates)[:, :, None]
        total, held, hop, first = None, own_end, 1, None
        while hop < blocks:
            got = jnp.roll(shift(held.astype(BF16), sign * hop, False), sign * hop, axis=0).astype(F32)
            first = got if first is None else first
            total = got if total is None else total + fade ** (hop - 1) * got
            held = held + fade**hop * got
            hop *= 2
        return total, first

    inner, end = call(
        forward_kernel, (blocks,),
        value_part + [block((depth, tokens))] * 2 + [block((tokens, depth))] * 2 + common,
        [block((span, cw)), block((modes, cw))],
        [f32(blocks, span, cw), f32(blocks, modes, cw)],
        scratch, flops=blocks * 10 * depth * span * cw, moved=blocks * span * cw * 8, name="forward",
    )(place, *vg, *af, *lf, taps, res, rate_col, skip)
    cots = [cotangent, swap(after(cotangent, end), 1), cot_y, swap(after(cot_y, end), 1)]
    coming, first = scan(end, 1)
    ring.append(shift(after(ring[-1], first), 1, True))
    for _ in range(blocks - len(ring)):
        ring.append(shift(ring[-1], 1, True))
    conv, mixed, turned = call(
        mixed_kernel, (blocks,),
        [block((modes, cw))] + gate_part + [block((span, cw))] + lead,
        [block((span, cw)), block((span, cw)), block((cw, span))],
        [f32(blocks, span, cw), b16(blocks, span, cw), b16(blocks, cw, span)],
        flops=blocks * 6 * span * cw * modes, moved=blocks * span * cw * 14, name="mixed",
    )(place, coming, *vg, inner, *lf, res, rate_col)
    wgrads = call(
        weight_kernel, (steps,),
        [whole((blocks, cw, span))] + [cols(tokens)] * LANES,
        [cols(cw)] * blocks, [f32(cw, width)] * hops + [b16(cw, width)],
        flops=2 * blocks * span * cw * width, moved=4 * span * width, name="weight",
    )(place, turned, *cots)
    part = shift(wgrads[-1], -1, True)

    def pass_on_sum(part, m):
        return shift((wgrads[m] + part.astype(F32)).astype(BF16), -1, True)

    keep, pass_on, send = call(
        functools.partial(output_kernel, blocks=blocks), (steps,),
        [whole((blocks, span, cw))] + [cols(cw)] * blocks,
        [cols(tokens), cols(tokens), pl.BlockSpec((2, tokens, tile), lambda i, *_: (0, 0, i))],
        [f32(tokens, width), f32(tokens, width), b16(2, tokens, width)],
        flops=2 * span * blocks * cw * width, moved=4 * width * blocks * cw, name="output",
    )(place, after(mixed, wgrads), *ring)
    near = swap(send, 1)
    far = swap((pass_on + near[1].astype(F32)).astype(BF16), 2)
    output = keep + near[0].astype(F32) + far.astype(F32)

    grad = call(
        functools.partial(grad_kernel, blocks=blocks), (steps,),
        [cols(cw)] * blocks + [cols(tokens)] * LANES,
        whole((blocks, span, cw)), f32(blocks, span, cw),
        flops=2 * blocks * span * cw * width, moved=4 * span * width, name="grad",
    )(place, *ring, *after(tuple(cots), wgrads))
    out = call(
        backward_kernel, (blocks,),
        gate_part + [block((span, cw))] * 2 + [block((depth, tokens))] * 2 + [block((tokens, depth))] * 2 + common,
        [block((tokens, cw))] * LANES + [block((span, cw)), block((modes, cw))],
        [b16(blocks, tokens, cw)] * LANES + [f32(blocks, span, cw), f32(blocks, modes, cw)],
        scratch, flops=blocks * 12 * depth * span * cw, moved=blocks * span * cw * 20, name="backward",
    )(place, *vg, grad, conv, *ab, *lb, taps, res, rate_col, skip)
    ggrads, inner_back, end_back = out[:LANES], out[LANES], out[LANES + 1]
    coming, first = scan(end_back, -1)
    part = pass_on_sum(after(part, end_back), blocks - 2)

    vgrads = call(
        value_kernel, (blocks,),
        [block((modes, cw))] + [block((span, cw))] + lead,
        [block((tokens, cw))] * LANES, [b16(blocks, tokens, cw)] * LANES,
        flops=blocks * 6 * span * cw * modes, moved=blocks * 6 * span * cw, name="value",
    )(place, coming, inner_back, *lb, res, rate_col)
    for m in range(blocks - 3, 0, -1):
        part = pass_on_sum(after(part, coming) if m == blocks - 3 else part, m)
    wgrad = wgrads[0] + part.astype(F32)
    gg = [ggrads[0]] + [swap(ggrads[s], s) for s in range(1, LANES)]
    vv = [vgrads[0]] + [swap(vgrads[s], s) for s in range(1, LANES)]
    if aligned:
        value_grad, gate_grad = call(
            functools.partial(unpack_kernel, blocks=blocks, width=cw), (1,),
            [whole((blocks, tokens, cw))] * (2 * LANES), [whole((tokens, width))] * 2,
            [b16(tokens, width)] * 2, moved=8 * tokens * width, name="unpack",
        )(place, *vv, *gg)
    else:

        def joined(pieces):
            full = by_slot(jnp.stack(by_lane(pieces), axis=1))
            return full.transpose(2, 0, 1, 3).reshape(tokens, width)

        value_grad, gate_grad = joined(vv), joined(gg)
    return output.astype(BF16), value_grad, gate_grad, wgrad


def solution(mesh):
    rows = P(("parts", "ctx"), None)
    return jax.shard_map(
        per_device,
        mesh=mesh,
        in_specs=(rows, rows, rows, P("parts", None), P("parts", None), P("parts"), rows),
        out_specs=(rows, rows, rows, rows),
        check_vma=False,
    )
```

```python
import functools

import jax
import jax.numpy as jnp
from jax import lax
from jax.experimental import pallas as pl
from jax.experimental.pallas import tpu as pltpu
from jax.sharding import PartitionSpec as P

SUB = 16
LANES = 4
BF16 = jnp.bfloat16
F32 = jnp.float32
VMEM_LIMIT = 32 * 1024 * 1024


def split(a):
    high = a.astype(BF16)
    return high, (a - high.astype(F32)).astype(BF16)


def dot(a, b, dims=((1,), (0,))):
    return lax.dot_general(a, b, (dims, ((), ())), preferred_element_type=F32)


def dot3(a_high, a_low, b):
    b_high, b_low = split(b)
    return dot(a_high, b_high) + dot(a_low, b_high) + dot(a_high, b_low)


def beside(parts):
    return jnp.concatenate(parts, axis=1)


def call(body, grid, in_specs, out_specs, out_shape, scratch=(), flops=0, moved=0, scalars=1, name=None):
    return pl.pallas_call(
        body,
        grid_spec=pltpu.PrefetchScalarGridSpec(
            num_scalar_prefetch=scalars,
            grid=grid,
            in_specs=in_specs,
            out_specs=out_specs,
            scratch_shapes=list(scratch),
        ),
        out_shape=out_shape,
        compiler_params=pltpu.CompilerParams(vmem_limit_bytes=VMEM_LIMIT),
        cost_estimate=pl.CostEstimate(flops=flops, bytes_accessed=moved, transcendentals=0),
        name=name,
    )


def whole(shape):
    return pl.BlockSpec(shape, lambda *_: (0,) * len(shape))


def block(shape, at=None):
    if at is None:
        return pl.BlockSpec((1,) + shape, lambda i, *_: (i,) + (0,) * len(shape))
    return pl.BlockSpec((1,) + shape, lambda *_: (at,) + (0,) * len(shape))


def powers_kernel(rate_col, rate_row, res, af_h, af_l, ab_h, ab_l, lf_h, lf_l, lb_h, lb_l, taps, *, tokens, modes):
    subs = tokens // SUB
    depth = subs * modes
    row = lax.broadcasted_iota(jnp.int32, (depth, tokens), 0) // modes
    tok = lax.broadcasted_iota(jnp.int32, (depth, tokens), 1)

    def power(steps, rate, valid):
        held = jnp.maximum(steps, 0).astype(F32)
        return jnp.where(valid, jnp.exp(-held * rate), 0.0)

    rc = rate_col[0]
    ahead = SUB * (row + 1) - 1 - tok
    af_h[0], af_l[0] = split(power(ahead, rc, ahead >= 0))
    behind = tok - SUB * row
    ab_h[0], ab_l[0] = split(power(behind, rc, behind >= 0))
    col = lax.broadcasted_iota(jnp.int32, (tokens, depth), 1) // modes
    out = lax.broadcasted_iota(jnp.int32, (tokens, depth), 0)
    inside = out % SUB
    rr = rate_row[0]
    carry = col == subs - 1
    steps = jnp.where(carry, out + 1, inside + 1)
    lf_h[0], lf_l[0] = split(power(steps, rr, carry | (out // SUB == col + 1)))
    carry = col == 0
    steps = jnp.where(carry, tokens - out, SUB - inside)
    lb_h[0], lb_l[0] = split(power(steps, rr, carry | (out // SUB == col - 1)))
    lag = lax.broadcasted_iota(jnp.int32, (SUB, modes), 0).astype(F32)
    taps[0] = lax.dot_general(
        jnp.exp(-lag * rr[:, :modes]),
        res[0],
        (((1,), (0,)), ((), ())),
        precision=lax.Precision.HIGHEST,
        preferred_element_type=F32,
    )


def inner_conv(xs, x_scr, e_scr, c_scr, inner, end, a_h, a_l, l_h, l_l, taps, res, rate_col, skip, lane, exact, back):
    tokens, width = xs[0].shape
    modes = res.shape[0]
    subs = tokens // SUB
    order = range(LANES - 1, -1, -1) if back else range(LANES)
    joined = width % 128 == 0
    groups = [list(range(LANES))] if joined else [[s] for s in range(LANES)]
    starts = [None] * LANES
    for group in groups:
        x = beside([xs[s] for s in group]) if len(group) > 1 else xs[group[0]]
        if exact:
            xh = x.astype(BF16)
            st = dot(a_h, xh) + dot(a_l, xh)
        else:
            st = dot3(a_h, a_l, x)
        for at, s in enumerate(group):
            starts[s] = st[:, at * width : (at + 1) * width]
    for s in range(LANES):
        part = starts[s]
        e_scr[s ^ lane] = part[:modes] if back else part[(subs - 1) * modes :]
    fade = jnp.exp(-float(tokens) * rate_col)
    state = jnp.zeros((modes, width), F32)
    for k in order:
        c_scr[k] = state
        state = fade * state + e_scr[k]
    end[...] = state
    weight = jnp.concatenate([res] * subs, axis=0)
    for group in groups:
        pieces = []
        for s in group:
            c = c_scr[s ^ lane]
            if back:
                full = jnp.concatenate([c, starts[s][modes:]], axis=0)
            else:
                full = jnp.concatenate([starts[s][: (subs - 1) * modes], c], axis=0)
            pieces.append(full * weight)
        w = beside(pieces) if len(pieces) > 1 else pieces[0]
        cross = dot3(l_h, l_l, w)
        for at, s in enumerate(group):
            inner[pl.ds(s * tokens, tokens), :] = cross[:, at * width : (at + 1) * width]
    row = lax.broadcasted_iota(jnp.int32, (SUB, width), 0)
    tap = taps + jnp.where(row == 0, skip, 0.0)
    spread = [jnp.broadcast_to(tap[k : k + 1, :], (subs, width)) for k in range(SUB)]
    for s in range(LANES):
        x_scr[...] = xs[s]
        held = [x_scr[pl.ds(t, subs, stride=SUB), :] for t in range(SUB)]
        for t in range(SUB):
            sources = range(t, SUB) if back else range(t + 1)
            total = None
            for u in sources:
                term = spread[abs(t - u)] * held[u]
                total = term if total is None else total + term
            at = pl.ds(s * tokens + t, subs, stride=SUB)
            inner[at, :] = inner[at, :] + total


def cross_conv(state, lead_h, lead_l, res, rate_col, lane, tokens, back):
    width = state.shape[1]
    weighted = state * res
    joined = width % 128 == 0
    parts = []
    for s in range(LANES):
        k = s ^ lane
        steps = ((LANES - 1 - k) if back else k).astype(F32) * float(tokens)
        parts.append(jnp.exp(-steps * rate_col) * weighted)
    if joined:
        cross = dot3(lead_h, lead_l, beside(parts))
        return [cross[:, s * width : (s + 1) * width] for s in range(LANES)]
    return [dot3(lead_h, lead_l, p) for p in parts]


def forward_kernel(place, *refs):
    xs = refs[:LANES]
    a_h, a_l, l_h, l_l, taps, res, rate_col, skip, inner, end, x_scr, e_scr, c_scr = refs[LANES:]
    modes = res.shape[1]
    inner_conv(
        [x[0, 0].astype(F32) for x in xs], x_scr, e_scr, c_scr, inner.at[0], end.at[0],
        a_h[0], a_l[0], l_h[0], l_l[0], taps[0], res[0], rate_col[0][:modes], skip[0], place[0], True, False,
    )


def mixed_kernel(place, coming, *refs):
    gates, refs = refs[:LANES], refs[LANES:]
    inner, l_h, l_l, res, rate_col, conv, mixed, turned = refs
    tokens = gates[0].shape[2]
    modes = res.shape[1]
    rate = rate_col[0][:modes]
    state = coming[0]
    depth = l_h.shape[2]
    parts = cross_conv(
        state, l_h[0][:, depth - modes :], l_l[0][:, depth - modes :], res[0], rate, place[0], tokens, False
    )
    for s in range(LANES):
        at = pl.ds(s * tokens, tokens)
        value = inner[0, at, :] + parts[s]
        conv[0, at, :] = value
        product = gates[s][0, 0].astype(F32) * value
        mixed[0, at, :] = product.astype(BF16)
        turned[0, :, s * tokens : (s + 1) * tokens] = product.T.astype(BF16)


def weight_kernel(place, turned, *refs):
    cots, outs = refs[:LANES], refs[LANES:]
    right = jnp.concatenate([cot[...] for cot in cots], axis=0)
    for m, out in enumerate(outs):
        out[...] = dot(turned[m], right).astype(out.dtype)


def grad_kernel(place, *refs, blocks):
    weights, cots, grad = refs[:blocks], refs[blocks : blocks + LANES], refs[-1]
    left = jnp.concatenate([cot[...] for cot in cots], axis=0)
    width = weights[0].shape[0]
    first = pl.program_id(0) == 0
    if width % 128 == 0:
        right = jnp.concatenate([w[...] for w in weights], axis=0)
        wide = dot(left, right, ((1,), (1,)))
        parts = [wide[:, m * width : (m + 1) * width] for m in range(blocks)]
    else:
        parts = [dot(left, w[...], ((1,), (1,))) for w in weights]

    @pl.when(first)
    def _():
        for m in range(blocks):
            grad[m] = parts[m]

    @pl.when(jnp.logical_not(first))
    def _():
        for m in range(blocks):
            grad[m] = grad[m] + parts[m]


def backward_kernel(place, *refs):
    gates, refs = refs[:LANES], refs[LANES:]
    grad, conv, a_h, a_l, l_h, l_l, taps, res, rate_col, skip = refs[:10]
    ggrads = refs[10 : 10 + LANES]
    inner, end, x_scr, e_scr, c_scr = refs[10 + LANES :]
    modes = res.shape[1]
    tokens = gates[0].shape[2]
    backs = []
    for s in range(LANES):
        at = pl.ds(s * tokens, tokens)
        g = grad[0, at, :]
        ggrads[s][0] = (g * conv[0, at, :]).astype(BF16)
        backs.append(g * gates[s][0, 0].astype(F32))
    inner_conv(
        backs, x_scr, e_scr, c_scr, inner.at[0], end.at[0],
        a_h[0], a_l[0], l_h[0], l_l[0], taps[0], res[0], rate_col[0][:modes], skip[0], place[0], False, True,
    )


def value_kernel(place, coming, *refs):
    inner, l_h, l_l, res, rate_col = refs[:5]
    outs = refs[5:]
    tokens = outs[0].shape[1]
    modes = res.shape[1]
    rate = rate_col[0][:modes]
    state = coming[0]
    parts = cross_conv(state, l_h[0][:, :modes], l_l[0][:, :modes], res[0], rate, place[0], tokens, True)
    for s in range(LANES):
        outs[s][0] = (inner[0, pl.ds(s * tokens, tokens), :] + parts[s]).astype(BF16)


def output_kernel(place, mixed, *refs, blocks):
    weights, (keep, pass_on, send) = refs[:blocks], refs[blocks:]
    tokens = keep.shape[0]
    width = mixed.shape[2]
    if width % 128 == 0:
        left = beside([mixed[m] for m in range(blocks)])
        right = jnp.concatenate([w[...] for w in weights], axis=0)
        total = dot(left, right)
    else:
        total = 0.0
        for m in range(blocks):
            total = total + dot(mixed[m], weights[m][...])
    keep[...] = total[:tokens]
    send[0] = total[tokens : 2 * tokens].astype(BF16)
    pass_on[...] = total[2 * tokens : 3 * tokens]
    send[1] = total[3 * tokens :].astype(BF16)


def pack_kernel(place, *refs, blocks, width):
    lane, turn = place[0], place[1]
    xs, outs = refs[:2], refs[2:]
    for s in range(LANES):
        for m in range(blocks):
            at = lax.rem(turn - m + blocks, blocks) * LANES + (s ^ lane)
            for which in range(2):
                outs[s][which, m] = xs[which][:, pl.ds(pl.multiple_of(at * width, width), width)]


def unpack_kernel(place, *refs, blocks, width):
    lane, turn = place[0], place[1]
    outs = refs[-2:]
    for which in range(2):
        for s in range(LANES):
            piece = refs[which * LANES + s]
            for m in range(blocks):
                at = lax.rem(turn - m + blocks, blocks) * LANES + (s ^ lane)
                outs[which][:, pl.ds(pl.multiple_of(at * width, width), width)] = piece[m]


def per_device(values, gating, out_weight, residue, decay_rate, skip_gain, cotangent):
    tokens, width = values.shape
    groups, modes = decay_rate.shape
    count = lax.axis_size("ctx")
    blocks = count // LANES
    cw = width // count
    span = LANES * tokens
    subs = tokens // SUB
    depth = subs * modes
    hops = blocks - 1
    me = lax.axis_index("ctx")
    lane, turn = lax.rem(me, LANES), me // LANES
    place = jnp.stack([lane, turn]).astype(jnp.int32)
    tile = min(512, width)
    steps = width // tile

    def swap(x, s):
        return lax.ppermute(x, "ctx", [(i, i ^ s) for i in range(count)])

    def shift(x, hop, wrap):
        pairs = []
        for i in range(count):
            to = i + hop * LANES
            if wrap:
                pairs.append((i, to % count))
            elif 0 <= to < count:
                pairs.append((i, to))
        return lax.ppermute(x, "ctx", pairs)

    def after(x, *others):
        return lax.optimization_barrier((x,) + others)[0]

    f32 = lambda *s: jax.ShapeDtypeStruct(s, F32)
    b16 = lambda *s: jax.ShapeDtypeStruct(s, BF16)

    def by_slot(x):
        turned = x[::-1]
        return lax.dynamic_slice_in_dim(jnp.concatenate([turned, turned]), blocks - 1 - turn, blocks, 0)

    def by_lane(pieces):
        one = jnp.bitwise_and(lane, 1) == 1
        two = jnp.bitwise_and(lane, 2) == 2
        pieces = [jnp.where(one, pieces[s ^ 1], pieces[s]) for s in range(LANES)]
        return [jnp.where(two, pieces[s ^ 2], pieces[s]) for s in range(LANES)]

    aligned = cw % 128 == 0
    if aligned:
        sent = call(
            functools.partial(pack_kernel, blocks=blocks, width=cw),
            (1,), [whole((tokens, width))] * 2, [whole((2, blocks, tokens, cw))] * LANES,
            [b16(2, blocks, tokens, cw)] * LANES, moved=8 * tokens * width, name="pack",
        )(place, values, gating)
    else:

        def parts(x):
            return by_slot(x.reshape(tokens, blocks, LANES, cw).transpose(1, 2, 0, 3))

        pv, pg = parts(values), parts(gating)
        sent = by_lane([jnp.stack([pv[:, s], pg[:, s]]) for s in range(LANES)])
    def own(x):
        x = x.reshape((blocks, LANES) + x.shape[1:])
        return by_slot(lax.dynamic_index_in_dim(x, lane, 1, False))

    rate = decay_rate / float(tokens * count)
    rates = own(jnp.repeat(rate, count // groups, axis=0))
    res = own(residue.reshape(count, cw, modes)).transpose(0, 2, 1)
    skip = own(skip_gain.reshape(count, cw))[:, None, :]
    tiled = jnp.tile(rates, (1, subs))
    rate_col, rate_row = tiled[:, :, None], tiled[:, None, :]
    powers = call(
        lambda place, *refs: powers_kernel(*refs, tokens=tokens, modes=modes),
        (blocks,),
        [block((depth, 1)), block((1, depth)), block((modes, cw))],
        [block((depth, tokens))] * 4 + [block((tokens, depth))] * 4 + [block((SUB, cw))],
        [b16(blocks, depth, tokens)] * 4 + [b16(blocks, tokens, depth)] * 4 + [f32(blocks, SUB, cw)],
        moved=blocks * depth * tokens * 16, name="powers",
    )(place, rate_col, rate_row, res)
    af, ab, lf, lb, taps = powers[0:2], powers[2:4], powers[4:6], powers[6:8], powers[8]

    ring = [out_weight, shift(out_weight, 1, True)]
    vg = [sent[0]] + [swap(sent[s], s) for s in (2, 3, 1)]
    vg = [vg[0], vg[3], vg[1], vg[2]]
    cot_y = swap(after(cotangent, taps, *vg[1:]), 2)
    ring.append(shift(after(ring[-1], taps, *vg[1:]), 1, True))

    scratch = [
        pltpu.VMEM((tokens, cw), F32),
        pltpu.VMEM((LANES, modes, cw), F32),
        pltpu.VMEM((LANES, modes, cw), F32),
    ]
    common = [block((SUB, cw)), block((modes, cw)), block((depth, 1)), block((1, cw))]
    lead = [block((tokens, depth))] * 2 + [block((modes, cw)), block((depth, 1))]
    value_part = [pl.BlockSpec((1, 1, tokens, cw), lambda i, *_: (0, i, 0, 0))] * LANES
    gate_part = [pl.BlockSpec((1, 1, tokens, cw), lambda i, *_: (1, i, 0, 0))] * LANES
    cols = lambda r: pl.BlockSpec((r, tile), lambda i, *_: (0, i))

    def scan(own_end, sign, doubling):
        fade = jnp.exp(-float(span) * rates)[:, :, None]
        total, held, hop, first = None, own_end, 1, None
        while hop < blocks:
            got = jnp.roll(shift(held.astype(BF16), sign * hop, False), sign * hop, axis=0).astype(F32)
            first = got if first is None else first
            total = got if total is None else total + fade ** (hop - 1) * got
            if doubling:
                held = held + fade**hop * got
                hop *= 2
            else:
                hop += 1
        return total, first

    inner, end = call(
        forward_kernel, (blocks,),
        value_part + [block((depth, tokens))] * 2 + [block((tokens, depth))] * 2 + common,
        [block((span, cw)), block((modes, cw))],
        [f32(blocks, span, cw), f32(blocks, modes, cw)],
        scratch, flops=blocks * 10 * depth * span * cw, moved=blocks * span * cw * 8, name="forward",
    )(place, *vg, *af, *lf, taps, res, rate_col, skip)
    cots = [cotangent, swap(after(cotangent, end), 1), cot_y, swap(after(cot_y, end), 1)]
    coming, first = scan(end, 1, True)
    ring.append(shift(after(ring[-1], first), 1, True))
    for _ in range(blocks - len(ring)):
        ring.append(shift(ring[-1], 1, True))
    conv, mixed, turned = call(
        mixed_kernel, (blocks,),
        [block((modes, cw))] + gate_part + [block((span, cw))] + lead,
        [block((span, cw)), block((span, cw)), block((cw, span))],
        [f32(blocks, span, cw), b16(blocks, span, cw), b16(blocks, cw, span)],
        flops=blocks * 6 * span * cw * modes, moved=blocks * span * cw * 14, name="mixed",
    )(place, coming, *vg, inner, *lf, res, rate_col)
    wgrads = call(
        weight_kernel, (steps,),
        [whole((blocks, cw, span))] + [cols(tokens)] * LANES,
        [cols(cw)] * blocks, [f32(cw, width)] * hops + [b16(cw, width)],
        flops=2 * blocks * span * cw * width, moved=4 * span * width, name="weight",
    )(place, turned, *cots)
    part = shift(wgrads[-1], -1, True)

    def pass_on_sum(part, m):
        return shift((wgrads[m] + part.astype(F32)).astype(BF16), -1, True)

    keep, pass_on, send = call(
        functools.partial(output_kernel, blocks=blocks), (steps,),
        [whole((blocks, span, cw))] + [cols(cw)] * blocks,
        [cols(tokens), cols(tokens), pl.BlockSpec((2, tokens, tile), lambda i, *_: (0, 0, i))],
        [f32(tokens, width), f32(tokens, width), b16(2, tokens, width)],
        flops=2 * span * blocks * cw * width, moved=4 * width * blocks * cw, name="output",
    )(place, after(mixed, wgrads), *ring)
    near = swap(send, 1)
    far = swap((pass_on + near[1].astype(F32)).astype(BF16), 2)
    output = keep + near[0].astype(F32) + far.astype(F32)

    grad = call(
        functools.partial(grad_kernel, blocks=blocks), (steps,),
        [cols(cw)] * blocks + [cols(tokens)] * LANES,
        whole((blocks, span, cw)), f32(blocks, span, cw),
        flops=2 * blocks * span * cw * width, moved=4 * span * width, name="grad",
    )(place, *ring, *after(tuple(cots), wgrads))
    out = call(
        backward_kernel, (blocks,),
        gate_part + [block((span, cw))] * 2 + [block((depth, tokens))] * 2 + [block((tokens, depth))] * 2 + common,
        [block((tokens, cw))] * LANES + [block((span, cw)), block((modes, cw))],
        [b16(blocks, tokens, cw)] * LANES + [f32(blocks, span, cw), f32(blocks, modes, cw)],
        scratch, flops=blocks * 12 * depth * span * cw, moved=blocks * span * cw * 20, name="backward",
    )(place, *vg, after(grad, near), conv, *ab, *lb, taps, res, rate_col, skip)
    ggrads, inner_back, end_back = out[:LANES], out[LANES], out[LANES + 1]
    coming, first = scan(end_back, -1, blocks > 4)
    part = pass_on_sum(after(part, end_back), blocks - 2)

    vgrads = call(
        value_kernel, (blocks,),
        [block((modes, cw))] + [block((span, cw))] + lead,
        [block((tokens, cw))] * LANES, [b16(blocks, tokens, cw)] * LANES,
        flops=blocks * 6 * span * cw * modes, moved=blocks * 6 * span * cw, name="value",
    )(place, after(coming, far), inner_back, *lb, res, rate_col)
    for m in range(blocks - 3, 0, -1):
        part = pass_on_sum(after(part, vgrads[0]) if m == blocks - 3 else part, m)
    wgrad = wgrads[0] + part.astype(F32)
    gg = [ggrads[0]] + [swap(ggrads[s], s) for s in range(1, LANES)]
    vv = [vgrads[0]] + [swap(vgrads[s], s) for s in range(1, LANES)]
    if aligned:
        value_grad, gate_grad = call(
            functools.partial(unpack_kernel, blocks=blocks, width=cw), (1,),
            [whole((blocks, tokens, cw))] * (2 * LANES), [whole((tokens, width))] * 2,
            [b16(tokens, width)] * 2, moved=8 * tokens * width, name="unpack",
        )(place, *vv, *gg)
    else:

        def joined(pieces):
            full = by_slot(jnp.stack(by_lane(pieces), axis=1))
            return full.transpose(2, 0, 1, 3).reshape(tokens, width)

        value_grad, gate_grad = joined(vv), joined(gg)
    return output.astype(BF16), value_grad, gate_grad, wgrad


def solution(mesh):
    rows = P(("parts", "ctx"), None)
    return jax.shard_map(
        per_device,
        mesh=mesh,
        in_specs=(rows, rows, rows, P("parts", None), P("parts", None), P("parts"), rows),
        out_specs=(rows, rows, rows, rows),
        check_vma=False,
    )
```

```python
import functools

import jax
import jax.numpy as jnp
from jax import lax
from jax.experimental import pallas as pl
from jax.experimental.pallas import tpu as pltpu
from jax.sharding import PartitionSpec as P

SUB = 16
LANES = 4
BF16 = jnp.bfloat16
F32 = jnp.float32
VMEM_LIMIT = 32 * 1024 * 1024


def split(a):
    high = a.astype(BF16)
    return high, (a - high.astype(F32)).astype(BF16)


def dot(a, b, dims=((1,), (0,))):
    return lax.dot_general(a, b, (dims, ((), ())), preferred_element_type=F32)


def dot3(a_high, a_low, b):
    b_high, b_low = split(b)
    return dot(a_high, b_high) + dot(a_low, b_high) + dot(a_high, b_low)


def beside(parts):
    return jnp.concatenate(parts, axis=1)


def call(body, grid, in_specs, out_specs, out_shape, scratch=(), flops=0, moved=0, scalars=1, name=None):
    return pl.pallas_call(
        body,
        grid_spec=pltpu.PrefetchScalarGridSpec(
            num_scalar_prefetch=scalars,
            grid=grid,
            in_specs=in_specs,
            out_specs=out_specs,
            scratch_shapes=list(scratch),
        ),
        out_shape=out_shape,
        compiler_params=pltpu.CompilerParams(vmem_limit_bytes=VMEM_LIMIT),
        cost_estimate=pl.CostEstimate(flops=flops, bytes_accessed=moved, transcendentals=0),
        name=name,
    )


def whole(shape):
    return pl.BlockSpec(shape, lambda *_: (0,) * len(shape))


def block(shape, at=None):
    if at is None:
        return pl.BlockSpec((1,) + shape, lambda i, *_: (i,) + (0,) * len(shape))
    return pl.BlockSpec((1,) + shape, lambda *_: (at,) + (0,) * len(shape))


def powers_kernel(rate_col, rate_row, res, af_h, af_l, ab_h, ab_l, lf_h, lf_l, lb_h, lb_l, taps, *, tokens, modes):
    subs = tokens // SUB
    depth = subs * modes
    row = lax.broadcasted_iota(jnp.int32, (depth, tokens), 0) // modes
    tok = lax.broadcasted_iota(jnp.int32, (depth, tokens), 1)

    def power(steps, rate, valid):
        held = jnp.maximum(steps, 0).astype(F32)
        return jnp.where(valid, jnp.exp(-held * rate), 0.0)

    rc = rate_col[0]
    ahead = SUB * (row + 1) - 1 - tok
    af_h[0], af_l[0] = split(power(ahead, rc, ahead >= 0))
    behind = tok - SUB * row
    ab_h[0], ab_l[0] = split(power(behind, rc, behind >= 0))
    col = lax.broadcasted_iota(jnp.int32, (tokens, depth), 1) // modes
    out = lax.broadcasted_iota(jnp.int32, (tokens, depth), 0)
    inside = out % SUB
    rr = rate_row[0]
    carry = col == subs - 1
    steps = jnp.where(carry, out + 1, inside + 1)
    lf_h[0], lf_l[0] = split(power(steps, rr, carry | (out // SUB == col + 1)))
    carry = col == 0
    steps = jnp.where(carry, tokens - out, SUB - inside)
    lb_h[0], lb_l[0] = split(power(steps, rr, carry | (out // SUB == col - 1)))
    lag = lax.broadcasted_iota(jnp.int32, (SUB, modes), 0).astype(F32)
    taps[0] = lax.dot_general(
        jnp.exp(-lag * rr[:, :modes]),
        res[0],
        (((1,), (0,)), ((), ())),
        precision=lax.Precision.HIGHEST,
        preferred_element_type=F32,
    )


def inner_conv(xs, x_scr, e_scr, c_scr, inner, end, a_h, a_l, l_h, l_l, taps, res, rate_col, skip, lane, exact, back):
    tokens, width = xs[0].shape
    modes = res.shape[0]
    subs = tokens // SUB
    order = range(LANES - 1, -1, -1) if back else range(LANES)
    joined = width % 128 == 0
    groups = [list(range(LANES))] if joined else [[s] for s in range(LANES)]
    starts = [None] * LANES
    for group in groups:
        x = beside([xs[s] for s in group]) if len(group) > 1 else xs[group[0]]
        if exact:
            xh = x.astype(BF16)
            st = dot(a_h, xh) + dot(a_l, xh)
        else:
            st = dot3(a_h, a_l, x)
        for at, s in enumerate(group):
            starts[s] = st[:, at * width : (at + 1) * width]
    for s in range(LANES):
        part = starts[s]
        e_scr[s ^ lane] = part[:modes] if back else part[(subs - 1) * modes :]
    fade = jnp.exp(-float(tokens) * rate_col)
    state = jnp.zeros((modes, width), F32)
    for k in order:
        c_scr[k] = state
        state = fade * state + e_scr[k]
    end[...] = state
    weight = jnp.concatenate([res] * subs, axis=0)
    for group in groups:
        pieces = []
        for s in group:
            c = c_scr[s ^ lane]
            if back:
                full = jnp.concatenate([c, starts[s][modes:]], axis=0)
            else:
                full = jnp.concatenate([starts[s][: (subs - 1) * modes], c], axis=0)
            pieces.append(full * weight)
        w = beside(pieces) if len(pieces) > 1 else pieces[0]
        cross = dot3(l_h, l_l, w)
        for at, s in enumerate(group):
            inner[pl.ds(s * tokens, tokens), :] = cross[:, at * width : (at + 1) * width]
    row = lax.broadcasted_iota(jnp.int32, (SUB, width), 0)
    tap = taps + jnp.where(row == 0, skip, 0.0)
    spread = [jnp.broadcast_to(tap[k : k + 1, :], (subs, width)) for k in range(SUB)]
    for s in range(LANES):
        x_scr[...] = xs[s]
        held = [x_scr[pl.ds(t, subs, stride=SUB), :] for t in range(SUB)]
        for t in range(SUB):
            sources = range(t, SUB) if back else range(t + 1)
            total = None
            for u in sources:
                term = spread[abs(t - u)] * held[u]
                total = term if total is None else total + term
            at = pl.ds(s * tokens + t, subs, stride=SUB)
            inner[at, :] = inner[at, :] + total


def cross_conv(state, lead_h, lead_l, res, rate_col, lane, tokens, back):
    width = state.shape[1]
    weighted = state * res
    joined = width % 128 == 0
    parts = []
    for s in range(LANES):
        k = s ^ lane
        steps = ((LANES - 1 - k) if back else k).astype(F32) * float(tokens)
        parts.append(jnp.exp(-steps * rate_col) * weighted)
    if joined:
        cross = dot3(lead_h, lead_l, beside(parts))
        return [cross[:, s * width : (s + 1) * width] for s in range(LANES)]
    return [dot3(lead_h, lead_l, p) for p in parts]


def forward_kernel(place, *refs):
    xs = refs[:LANES]
    a_h, a_l, l_h, l_l, taps, res, rate_col, skip, inner, end, x_scr, e_scr, c_scr = refs[LANES:]
    modes = res.shape[1]
    inner_conv(
        [x[0, 0].astype(F32) for x in xs], x_scr, e_scr, c_scr, inner.at[0], end.at[0],
        a_h[0], a_l[0], l_h[0], l_l[0], taps[0], res[0], rate_col[0][:modes], skip[0], place[0], True, False,
    )


def mixed_kernel(place, coming, *refs):
    gates, refs = refs[:LANES], refs[LANES:]
    inner, l_h, l_l, res, rate_col, conv, mixed, turned = refs
    tokens = gates[0].shape[2]
    modes = res.shape[1]
    rate = rate_col[0][:modes]
    state = coming[0]
    depth = l_h.shape[2]
    parts = cross_conv(
        state, l_h[0][:, depth - modes :], l_l[0][:, depth - modes :], res[0], rate, place[0], tokens, False
    )
    for s in range(LANES):
        at = pl.ds(s * tokens, tokens)
        value = inner[0, at, :] + parts[s]
        conv[0, at, :] = value
        product = gates[s][0, 0].astype(F32) * value
        mixed[0, at, :] = product.astype(BF16)
        turned[0, :, s * tokens : (s + 1) * tokens] = product.T.astype(BF16)


def weight_kernel(place, turned, *refs):
    cots, outs = refs[:LANES], refs[LANES:]
    right = jnp.concatenate([cot[...] for cot in cots], axis=0)
    for m, out in enumerate(outs):
        out[...] = dot(turned[m], right).astype(out.dtype)


def grad_kernel(place, *refs, blocks):
    weights, cots, grad = refs[:blocks], refs[blocks : blocks + LANES], refs[-1]
    left = jnp.concatenate([cot[...] for cot in cots], axis=0)
    width = weights[0].shape[0]
    first = pl.program_id(0) == 0
    if width % 128 == 0:
        right = jnp.concatenate([w[...] for w in weights], axis=0)
        wide = dot(left, right, ((1,), (1,)))
        parts = [wide[:, m * width : (m + 1) * width] for m in range(blocks)]
    else:
        parts = [dot(left, w[...], ((1,), (1,))) for w in weights]

    @pl.when(first)
    def _():
        for m in range(blocks):
            grad[m] = parts[m]

    @pl.when(jnp.logical_not(first))
    def _():
        for m in range(blocks):
            grad[m] = grad[m] + parts[m]


def backward_kernel(place, *refs):
    gates, refs = refs[:LANES], refs[LANES:]
    grad, conv, a_h, a_l, l_h, l_l, taps, res, rate_col, skip = refs[:10]
    ggrads = refs[10 : 10 + LANES]
    inner, end, x_scr, e_scr, c_scr = refs[10 + LANES :]
    modes = res.shape[1]
    tokens = gates[0].shape[2]
    backs = []
    for s in range(LANES):
        at = pl.ds(s * tokens, tokens)
        g = grad[0, at, :]
        ggrads[s][0] = (g * conv[0, at, :]).astype(BF16)
        backs.append(g * gates[s][0, 0].astype(F32))
    inner_conv(
        backs, x_scr, e_scr, c_scr, inner.at[0], end.at[0],
        a_h[0], a_l[0], l_h[0], l_l[0], taps[0], res[0], rate_col[0][:modes], skip[0], place[0], False, True,
    )


def value_kernel(place, coming, *refs):
    inner, l_h, l_l, res, rate_col = refs[:5]
    outs = refs[5:]
    tokens = outs[0].shape[1]
    modes = res.shape[1]
    rate = rate_col[0][:modes]
    state = coming[0]
    parts = cross_conv(state, l_h[0][:, :modes], l_l[0][:, :modes], res[0], rate, place[0], tokens, True)
    for s in range(LANES):
        outs[s][0] = (inner[0, pl.ds(s * tokens, tokens), :] + parts[s]).astype(BF16)


def output_kernel(place, mixed, *refs, blocks):
    weights, (keep, pass_on, send) = refs[:blocks], refs[blocks:]
    tokens = keep.shape[0]
    width = mixed.shape[2]
    if width % 128 == 0:
        left = beside([mixed[m] for m in range(blocks)])
        right = jnp.concatenate([w[...] for w in weights], axis=0)
        total = dot(left, right)
    else:
        total = 0.0
        for m in range(blocks):
            total = total + dot(mixed[m], weights[m][...])
    keep[...] = total[:tokens]
    send[0] = total[tokens : 2 * tokens].astype(BF16)
    pass_on[...] = total[2 * tokens : 3 * tokens]
    send[1] = total[3 * tokens :].astype(BF16)


def pack_kernel(place, *refs, blocks, width):
    lane, turn = place[0], place[1]
    xs, outs = refs[:-LANES], refs[-LANES:]
    for s in range(LANES):
        for m in range(blocks):
            at = lax.rem(turn - m + blocks, blocks) * LANES + (s ^ lane)
            for which in range(len(xs)):
                outs[s][which, m] = xs[which][:, pl.ds(pl.multiple_of(at * width, width), width)]


def unpack_kernel(place, *refs, blocks, width):
    lane, turn = place[0], place[1]
    outs = refs[-2:]
    for which in range(2):
        for s in range(LANES):
            piece = refs[which * LANES + s]
            for m in range(blocks):
                at = lax.rem(turn - m + blocks, blocks) * LANES + (s ^ lane)
                outs[which][:, pl.ds(pl.multiple_of(at * width, width), width)] = piece[m]


def per_device(values, gating, out_weight, residue, decay_rate, skip_gain, cotangent):
    tokens, width = values.shape
    groups, modes = decay_rate.shape
    count = lax.axis_size("ctx")
    blocks = count // LANES
    cw = width // count
    span = LANES * tokens
    subs = tokens // SUB
    depth = subs * modes
    hops = blocks - 1
    me = lax.axis_index("ctx")
    lane, turn = lax.rem(me, LANES), me // LANES
    place = jnp.stack([lane, turn]).astype(jnp.int32)
    tile = min(512, width)
    steps = width // tile

    def swap(x, s):
        return lax.ppermute(x, "ctx", [(i, i ^ s) for i in range(count)])

    def shift(x, hop, wrap):
        pairs = []
        for i in range(count):
            to = i + hop * LANES
            if wrap:
                pairs.append((i, to % count))
            elif 0 <= to < count:
                pairs.append((i, to))
        return lax.ppermute(x, "ctx", pairs)

    def after(x, *others):
        return lax.optimization_barrier((x,) + others)[0]

    f32 = lambda *s: jax.ShapeDtypeStruct(s, F32)
    b16 = lambda *s: jax.ShapeDtypeStruct(s, BF16)

    def by_slot(x):
        turned = x[::-1]
        return lax.dynamic_slice_in_dim(jnp.concatenate([turned, turned]), blocks - 1 - turn, blocks, 0)

    def by_lane(pieces):
        one = jnp.bitwise_and(lane, 1) == 1
        two = jnp.bitwise_and(lane, 2) == 2
        pieces = [jnp.where(one, pieces[s ^ 1], pieces[s]) for s in range(LANES)]
        return [jnp.where(two, pieces[s ^ 2], pieces[s]) for s in range(LANES)]

    aligned = cw % 128 == 0
    def pack(x):
        if aligned:
            return call(
                functools.partial(pack_kernel, blocks=blocks, width=cw),
                (1,), [whole((tokens, width))], [whole((1, blocks, tokens, cw))] * LANES,
                [b16(1, blocks, tokens, cw)] * LANES, moved=4 * tokens * width, name="pack",
            )(place, x)
        pieces = by_slot(x.reshape(tokens, blocks, LANES, cw).transpose(1, 2, 0, 3))
        return by_lane([pieces[None, :, s] for s in range(LANES)])

    sent = pack(values)

    def own(x):
        x = x.reshape((blocks, LANES) + x.shape[1:])
        return by_slot(lax.dynamic_index_in_dim(x, lane, 1, False))

    rate = decay_rate / float(tokens * count)
    rates = own(jnp.repeat(rate, count // groups, axis=0))
    res = own(residue.reshape(count, cw, modes)).transpose(0, 2, 1)
    skip = own(skip_gain.reshape(count, cw))[:, None, :]
    tiled = jnp.tile(rates, (1, subs))
    rate_col, rate_row = tiled[:, :, None], tiled[:, None, :]
    powers = call(
        lambda place, *refs: powers_kernel(*refs, tokens=tokens, modes=modes),
        (blocks,),
        [block((depth, 1)), block((1, depth)), block((modes, cw))],
        [block((depth, tokens))] * 4 + [block((tokens, depth))] * 4 + [block((SUB, cw))],
        [b16(blocks, depth, tokens)] * 4 + [b16(blocks, tokens, depth)] * 4 + [f32(blocks, SUB, cw)],
        moved=blocks * depth * tokens * 16, name="powers",
    )(place, rate_col, rate_row, res)
    af, ab, lf, lb, taps = powers[0:2], powers[2:4], powers[4:6], powers[6:8], powers[8]

    ring = [out_weight, shift(out_weight, 1, True)]
    vs = {s: swap(sent[s], s) for s in (2, 3, 1)}
    vs = [sent[0]] + [vs[s] for s in range(1, LANES)]
    gates = pack(after(gating, *vs[1:]))
    gs = [gates[0]] + [swap(gates[s], s) for s in range(1, LANES)]
    cot_y = swap(after(cotangent, taps, *vs[1:]), 2)
    ring.append(shift(after(ring[-1], *vs[1:]), 1, True))

    scratch = [
        pltpu.VMEM((tokens, cw), F32),
        pltpu.VMEM((LANES, modes, cw), F32),
        pltpu.VMEM((LANES, modes, cw), F32),
    ]
    common = [block((SUB, cw)), block((modes, cw)), block((depth, 1)), block((1, cw))]
    lead = [block((tokens, depth))] * 2 + [block((modes, cw)), block((depth, 1))]
    value_part = [pl.BlockSpec((1, 1, tokens, cw), lambda i, *_: (0, i, 0, 0))] * LANES
    gate_part = [pl.BlockSpec((1, 1, tokens, cw), lambda i, *_: (0, i, 0, 0))] * LANES
    cols = lambda r: pl.BlockSpec((r, tile), lambda i, *_: (0, i))

    def scan(own_end, sign, doubling):
        fade = jnp.exp(-float(span) * rates)[:, :, None]
        total, held, hop, first = None, own_end, 1, None
        while hop < blocks:
            got = jnp.roll(shift(held.astype(BF16), sign * hop, False), sign * hop, axis=0).astype(F32)
            first = got if first is None else first
            total = got if total is None else total + fade ** (hop - 1) * got
            if doubling:
                held = held + fade**hop * got
                hop *= 2
            else:
                hop += 1
        return total, first

    inner, end = call(
        forward_kernel, (blocks,),
        value_part + [block((depth, tokens))] * 2 + [block((tokens, depth))] * 2 + common,
        [block((span, cw)), block((modes, cw))],
        [f32(blocks, span, cw), f32(blocks, modes, cw)],
        scratch, flops=blocks * 10 * depth * span * cw, moved=blocks * span * cw * 8, name="forward",
    )(place, *vs, *af, *lf, taps, res, rate_col, skip)
    cots = [cotangent, swap(after(cotangent, end), 1), cot_y, swap(after(cot_y, end), 1)]
    coming, first = scan(end, 1, True)
    ring.append(shift(after(ring[-1], first), 1, True))
    for _ in range(blocks - len(ring)):
        ring.append(shift(ring[-1], 1, True))
    conv, mixed, turned = call(
        mixed_kernel, (blocks,),
        [block((modes, cw))] + gate_part + [block((span, cw))] + lead,
        [block((span, cw)), block((span, cw)), block((cw, span))],
        [f32(blocks, span, cw), b16(blocks, span, cw), b16(blocks, cw, span)],
        flops=blocks * 6 * span * cw * modes, moved=blocks * span * cw * 14, name="mixed",
    )(place, coming, *gs, inner, *lf, res, rate_col)
    wgrads = call(
        weight_kernel, (steps,),
        [whole((blocks, cw, span))] + [cols(tokens)] * LANES,
        [cols(cw)] * blocks, [f32(cw, width)] * hops + [b16(cw, width)],
        flops=2 * blocks * span * cw * width, moved=4 * span * width, name="weight",
    )(place, turned, *cots)
    part = shift(wgrads[-1], -1, True)

    def pass_on_sum(part, m):
        return shift((wgrads[m] + part.astype(F32)).astype(BF16), -1, True)

    keep, pass_on, send = call(
        functools.partial(output_kernel, blocks=blocks), (steps,),
        [whole((blocks, span, cw))] + [cols(cw)] * blocks,
        [cols(tokens), cols(tokens), pl.BlockSpec((2, tokens, tile), lambda i, *_: (0, 0, i))],
        [f32(tokens, width), f32(tokens, width), b16(2, tokens, width)],
        flops=2 * span * blocks * cw * width, moved=4 * width * blocks * cw, name="output",
    )(place, after(mixed, wgrads), *ring)
    near = swap(send, 1)
    far = swap((pass_on + near[1].astype(F32)).astype(BF16), 2)
    output = keep + near[0].astype(F32) + far.astype(F32)

    grad = call(
        functools.partial(grad_kernel, blocks=blocks), (steps,),
        [cols(cw)] * blocks + [cols(tokens)] * LANES,
        whole((blocks, span, cw)), f32(blocks, span, cw),
        flops=2 * blocks * span * cw * width, moved=4 * span * width, name="grad",
    )(place, *ring, *after(tuple(cots), wgrads))
    out = call(
        backward_kernel, (blocks,),
        gate_part + [block((span, cw))] * 2 + [block((depth, tokens))] * 2 + [block((tokens, depth))] * 2 + common,
        [block((tokens, cw))] * LANES + [block((span, cw)), block((modes, cw))],
        [b16(blocks, tokens, cw)] * LANES + [f32(blocks, span, cw), f32(blocks, modes, cw)],
        scratch, flops=blocks * 12 * depth * span * cw, moved=blocks * span * cw * 20, name="backward",
    )(place, *gs, after(grad, near), conv, *ab, *lb, taps, res, rate_col, skip)
    ggrads, inner_back, end_back = out[:LANES], out[LANES], out[LANES + 1]
    coming, first = scan(end_back, -1, blocks > 4)
    part = pass_on_sum(after(part, end_back), blocks - 2)

    vgrads = call(
        value_kernel, (blocks,),
        [block((modes, cw))] + [block((span, cw))] + lead,
        [block((tokens, cw))] * LANES, [b16(blocks, tokens, cw)] * LANES,
        flops=blocks * 6 * span * cw * modes, moved=blocks * 6 * span * cw, name="value",
    )(place, after(coming, far), inner_back, *lb, res, rate_col)
    for m in range(blocks - 3, 0, -1):
        part = pass_on_sum(after(part, vgrads[0]) if m == blocks - 3 else part, m)
    wgrad = wgrads[0] + part.astype(F32)
    gg = {s: swap(ggrads[s], s) for s in (2, 3, 1)}
    gg = [ggrads[0]] + [gg[s] for s in range(1, LANES)]
    vv = {s: swap(vgrads[s], s) for s in (2, 3, 1)}
    vv = [vgrads[0]] + [vv[s] for s in range(1, LANES)]
    if aligned:
        value_grad, gate_grad = call(
            functools.partial(unpack_kernel, blocks=blocks, width=cw), (1,),
            [whole((blocks, tokens, cw))] * (2 * LANES), [whole((tokens, width))] * 2,
            [b16(tokens, width)] * 2, moved=8 * tokens * width, name="unpack",
        )(place, *vv, *gg)
    else:

        def joined(pieces):
            full = by_slot(jnp.stack(by_lane(pieces), axis=1))
            return full.transpose(2, 0, 1, 3).reshape(tokens, width)

        value_grad, gate_grad = joined(vv), joined(gg)
    return output.astype(BF16), value_grad, gate_grad, wgrad


def solution(mesh):
    rows = P(("parts", "ctx"), None)
    return jax.shard_map(
        per_device,
        mesh=mesh,
        in_specs=(rows, rows, rows, P("parts", None), P("parts", None), P("parts"), rows),
        out_specs=(rows, rows, rows, rows),
        check_vma=False,
    )
```

```python
import functools

import jax
import jax.numpy as jnp
from jax import lax
from jax.experimental import pallas as pl
from jax.experimental.pallas import tpu as pltpu
from jax.sharding import PartitionSpec as P

SUB = 16
LANES = 4
BF16 = jnp.bfloat16
F32 = jnp.float32
VMEM_LIMIT = 32 * 1024 * 1024


def split(a):
    high = a.astype(BF16)
    return high, (a - high.astype(F32)).astype(BF16)


def dot(a, b, dims=((1,), (0,))):
    return lax.dot_general(a, b, (dims, ((), ())), preferred_element_type=F32)


def dot3(a_high, a_low, b):
    b_high, b_low = split(b)
    return dot(a_high, b_high) + dot(a_low, b_high) + dot(a_high, b_low)


def beside(parts):
    return jnp.concatenate(parts, axis=1)


def call(body, grid, in_specs, out_specs, out_shape, scratch=(), flops=0, moved=0, scalars=1, name=None):
    return pl.pallas_call(
        body,
        grid_spec=pltpu.PrefetchScalarGridSpec(
            num_scalar_prefetch=scalars,
            grid=grid,
            in_specs=in_specs,
            out_specs=out_specs,
            scratch_shapes=list(scratch),
        ),
        out_shape=out_shape,
        compiler_params=pltpu.CompilerParams(vmem_limit_bytes=VMEM_LIMIT),
        cost_estimate=pl.CostEstimate(flops=flops, bytes_accessed=moved, transcendentals=0),
        name=name,
    )


def whole(shape):
    return pl.BlockSpec(shape, lambda *_: (0,) * len(shape))


def block(shape, at=None):
    if at is None:
        return pl.BlockSpec((1,) + shape, lambda i, *_: (i,) + (0,) * len(shape))
    return pl.BlockSpec((1,) + shape, lambda *_: (at,) + (0,) * len(shape))


def powers_kernel(rate_col, rate_row, res, af_h, af_l, ab_h, ab_l, lf_h, lf_l, lb_h, lb_l, taps, *, tokens, modes):
    subs = tokens // SUB
    depth = subs * modes
    row = lax.broadcasted_iota(jnp.int32, (depth, tokens), 0) // modes
    tok = lax.broadcasted_iota(jnp.int32, (depth, tokens), 1)

    def power(steps, rate, valid):
        held = jnp.maximum(steps, 0).astype(F32)
        return jnp.where(valid, jnp.exp(-held * rate), 0.0)

    rc = rate_col[0]
    ahead = SUB * (row + 1) - 1 - tok
    af_h[0], af_l[0] = split(power(ahead, rc, ahead >= 0))
    behind = tok - SUB * row
    ab_h[0], ab_l[0] = split(power(behind, rc, behind >= 0))
    col = lax.broadcasted_iota(jnp.int32, (tokens, depth), 1) // modes
    out = lax.broadcasted_iota(jnp.int32, (tokens, depth), 0)
    inside = out % SUB
    rr = rate_row[0]
    carry = col == subs - 1
    steps = jnp.where(carry, out + 1, inside + 1)
    lf_h[0], lf_l[0] = split(power(steps, rr, carry | (out // SUB == col + 1)))
    carry = col == 0
    steps = jnp.where(carry, tokens - out, SUB - inside)
    lb_h[0], lb_l[0] = split(power(steps, rr, carry | (out // SUB == col - 1)))
    lag = lax.broadcasted_iota(jnp.int32, (SUB, modes), 0).astype(F32)
    taps[0] = lax.dot_general(
        jnp.exp(-lag * rr[:, :modes]),
        res[0],
        (((1,), (0,)), ((), ())),
        precision=lax.Precision.HIGHEST,
        preferred_element_type=F32,
    )


def inner_conv(xs, x_scr, e_scr, c_scr, inner, end, a_h, a_l, l_h, l_l, taps, res, rate_col, skip, lane, exact, back):
    tokens, width = xs[0].shape
    modes = res.shape[0]
    subs = tokens // SUB
    order = range(LANES - 1, -1, -1) if back else range(LANES)
    joined = width % 128 == 0
    groups = [list(range(LANES))] if joined else [[s] for s in range(LANES)]
    starts = [None] * LANES
    for group in groups:
        x = beside([xs[s] for s in group]) if len(group) > 1 else xs[group[0]]
        if exact:
            xh = x.astype(BF16)
            st = dot(a_h, xh) + dot(a_l, xh)
        else:
            st = dot3(a_h, a_l, x)
        for at, s in enumerate(group):
            starts[s] = st[:, at * width : (at + 1) * width]
    for s in range(LANES):
        part = starts[s]
        e_scr[s ^ lane] = part[:modes] if back else part[(subs - 1) * modes :]
    fade = jnp.exp(-float(tokens) * rate_col)
    state = jnp.zeros((modes, width), F32)
    for k in order:
        c_scr[k] = state
        state = fade * state + e_scr[k]
    end[...] = state
    weight = jnp.concatenate([res] * subs, axis=0)
    for group in groups:
        pieces = []
        for s in group:
            c = c_scr[s ^ lane]
            if back:
                full = jnp.concatenate([c, starts[s][modes:]], axis=0)
            else:
                full = jnp.concatenate([starts[s][: (subs - 1) * modes], c], axis=0)
            pieces.append(full * weight)
        w = beside(pieces) if len(pieces) > 1 else pieces[0]
        cross = dot3(l_h, l_l, w)
        for at, s in enumerate(group):
            inner[pl.ds(s * tokens, tokens), :] = cross[:, at * width : (at + 1) * width]
    row = lax.broadcasted_iota(jnp.int32, (SUB, width), 0)
    tap = taps + jnp.where(row == 0, skip, 0.0)
    spread = [jnp.broadcast_to(tap[k : k + 1, :], (subs, width)) for k in range(SUB)]
    for s in range(LANES):
        x_scr[...] = xs[s]
        held = [x_scr[pl.ds(t, subs, stride=SUB), :] for t in range(SUB)]
        for t in range(SUB):
            sources = range(t, SUB) if back else range(t + 1)
            total = None
            for u in sources:
                term = spread[abs(t - u)] * held[u]
                total = term if total is None else total + term
            at = pl.ds(s * tokens + t, subs, stride=SUB)
            inner[at, :] = inner[at, :] + total


def cross_conv(state, lead_h, lead_l, res, rate_col, lane, tokens, back):
    width = state.shape[1]
    weighted = state * res
    joined = width % 128 == 0
    parts = []
    for s in range(LANES):
        k = s ^ lane
        steps = ((LANES - 1 - k) if back else k).astype(F32) * float(tokens)
        parts.append(jnp.exp(-steps * rate_col) * weighted)
    if joined:
        cross = dot3(lead_h, lead_l, beside(parts))
        return [cross[:, s * width : (s + 1) * width] for s in range(LANES)]
    return [dot3(lead_h, lead_l, p) for p in parts]


def forward_kernel(place, *refs):
    xs = refs[:LANES]
    a_h, a_l, l_h, l_l, taps, res, rate_col, skip, inner, end, x_scr, e_scr, c_scr = refs[LANES:]
    modes = res.shape[1]
    inner_conv(
        [x[0, 0].astype(F32) for x in xs], x_scr, e_scr, c_scr, inner.at[0], end.at[0],
        a_h[0], a_l[0], l_h[0], l_l[0], taps[0], res[0], rate_col[0][:modes], skip[0], place[0], True, False,
    )


def mixed_kernel(place, coming, *refs):
    gates, refs = refs[:LANES], refs[LANES:]
    inner, l_h, l_l, res, rate_col, conv, mixed, turned = refs
    tokens = gates[0].shape[2]
    modes = res.shape[1]
    rate = rate_col[0][:modes]
    state = coming[0]
    depth = l_h.shape[2]
    parts = cross_conv(
        state, l_h[0][:, depth - modes :], l_l[0][:, depth - modes :], res[0], rate, place[0], tokens, False
    )
    for s in range(LANES):
        at = pl.ds(s * tokens, tokens)
        value = inner[0, at, :] + parts[s]
        conv[0, at, :] = value
        product = gates[s][0, 0].astype(F32) * value
        mixed[0, at, :] = product.astype(BF16)
        turned[0, :, s * tokens : (s + 1) * tokens] = product.T.astype(BF16)


def weight_kernel(place, turned, *refs):
    cots, outs = refs[:LANES], refs[LANES:]
    right = jnp.concatenate([cot[...] for cot in cots], axis=0)
    for m, out in enumerate(outs):
        out[...] = dot(turned[m], right).astype(out.dtype)


def grad_kernel(place, *refs, blocks):
    weights, cots, grad = refs[:blocks], refs[blocks : blocks + LANES], refs[-1]
    left = jnp.concatenate([cot[...] for cot in cots], axis=0)
    width = weights[0].shape[0]
    first = pl.program_id(0) == 0
    if width % 128 == 0:
        right = jnp.concatenate([w[...] for w in weights], axis=0)
        wide = dot(left, right, ((1,), (1,)))
        parts = [wide[:, m * width : (m + 1) * width] for m in range(blocks)]
    else:
        parts = [dot(left, w[...], ((1,), (1,))) for w in weights]

    @pl.when(first)
    def _():
        for m in range(blocks):
            grad[m] = parts[m]

    @pl.when(jnp.logical_not(first))
    def _():
        for m in range(blocks):
            grad[m] = grad[m] + parts[m]


def backward_kernel(place, *refs):
    gates, refs = refs[:LANES], refs[LANES:]
    grad, conv, a_h, a_l, l_h, l_l, taps, res, rate_col, skip = refs[:10]
    ggrads = refs[10 : 10 + LANES]
    inner, end, x_scr, e_scr, c_scr = refs[10 + LANES :]
    modes = res.shape[1]
    tokens = gates[0].shape[2]
    backs = []
    for s in range(LANES):
        at = pl.ds(s * tokens, tokens)
        g = grad[0, at, :]
        ggrads[s][0] = (g * conv[0, at, :]).astype(BF16)
        backs.append(g * gates[s][0, 0].astype(F32))
    inner_conv(
        backs, x_scr, e_scr, c_scr, inner.at[0], end.at[0],
        a_h[0], a_l[0], l_h[0], l_l[0], taps[0], res[0], rate_col[0][:modes], skip[0], place[0], False, True,
    )


def value_kernel(place, coming, *refs):
    inner, l_h, l_l, res, rate_col = refs[:5]
    outs = refs[5:]
    tokens = outs[0].shape[1]
    modes = res.shape[1]
    rate = rate_col[0][:modes]
    state = coming[0]
    parts = cross_conv(state, l_h[0][:, :modes], l_l[0][:, :modes], res[0], rate, place[0], tokens, True)
    for s in range(LANES):
        outs[s][0] = (inner[0, pl.ds(s * tokens, tokens), :] + parts[s]).astype(BF16)


def output_kernel(place, mixed, *refs, blocks):
    weights, (keep, pass_on, send) = refs[:blocks], refs[blocks:]
    tokens = keep.shape[0]
    width = mixed.shape[2]
    if width % 128 == 0:
        left = beside([mixed[m] for m in range(blocks)])
        right = jnp.concatenate([w[...] for w in weights], axis=0)
        total = dot(left, right)
    else:
        total = 0.0
        for m in range(blocks):
            total = total + dot(mixed[m], weights[m][...])
    keep[...] = total[:tokens]
    send[0] = total[tokens : 2 * tokens].astype(BF16)
    pass_on[...] = total[2 * tokens : 3 * tokens]
    send[1] = total[3 * tokens :].astype(BF16)


def pack_kernel(place, *refs, blocks, width):
    lane, turn = place[0], place[1]
    xs, outs = refs[:-LANES], refs[-LANES:]
    for s in range(LANES):
        for m in range(blocks):
            at = lax.rem(turn - m + blocks, blocks) * LANES + (s ^ lane)
            for which in range(len(xs)):
                outs[s][which, m] = xs[which][:, pl.ds(pl.multiple_of(at * width, width), width)]


def unpack_kernel(place, *refs, blocks, width):
    lane, turn = place[0], place[1]
    outs = refs[-2:]
    for which in range(2):
        for s in range(LANES):
            piece = refs[which * LANES + s]
            for m in range(blocks):
                at = lax.rem(turn - m + blocks, blocks) * LANES + (s ^ lane)
                outs[which][:, pl.ds(pl.multiple_of(at * width, width), width)] = piece[m]


def per_device(values, gating, out_weight, residue, decay_rate, skip_gain, cotangent):
    tokens, width = values.shape
    groups, modes = decay_rate.shape
    count = lax.axis_size("ctx")
    blocks = count // LANES
    cw = width // count
    span = LANES * tokens
    subs = tokens // SUB
    depth = subs * modes
    hops = blocks - 1
    me = lax.axis_index("ctx")
    lane, turn = lax.rem(me, LANES), me // LANES
    place = jnp.stack([lane, turn]).astype(jnp.int32)
    tile = min(512, width)
    steps = width // tile

    def swap(x, s):
        return lax.ppermute(x, "ctx", [(i, i ^ s) for i in range(count)])

    def shift(x, hop, wrap):
        pairs = []
        for i in range(count):
            to = i + hop * LANES
            if wrap:
                pairs.append((i, to % count))
            elif 0 <= to < count:
                pairs.append((i, to))
        return lax.ppermute(x, "ctx", pairs)

    def after(x, *others):
        return lax.optimization_barrier((x,) + others)[0]

    f32 = lambda *s: jax.ShapeDtypeStruct(s, F32)
    b16 = lambda *s: jax.ShapeDtypeStruct(s, BF16)

    def by_slot(x):
        turned = x[::-1]
        return lax.dynamic_slice_in_dim(jnp.concatenate([turned, turned]), blocks - 1 - turn, blocks, 0)

    def by_lane(pieces):
        one = jnp.bitwise_and(lane, 1) == 1
        two = jnp.bitwise_and(lane, 2) == 2
        pieces = [jnp.where(one, pieces[s ^ 1], pieces[s]) for s in range(LANES)]
        return [jnp.where(two, pieces[s ^ 2], pieces[s]) for s in range(LANES)]

    aligned = cw % 128 == 0
    def pack(x):
        if aligned:
            return call(
                functools.partial(pack_kernel, blocks=blocks, width=cw),
                (1,), [whole((tokens, width))], [whole((1, blocks, tokens, cw))] * LANES,
                [b16(1, blocks, tokens, cw)] * LANES, moved=4 * tokens * width, name="pack",
            )(place, x)
        pieces = by_slot(x.reshape(tokens, blocks, LANES, cw).transpose(1, 2, 0, 3))
        return by_lane([pieces[None, :, s] for s in range(LANES)])

    sent = pack(values)

    def own(x):
        x = x.reshape((blocks, LANES) + x.shape[1:])
        return by_slot(lax.dynamic_index_in_dim(x, lane, 1, False))

    rate = decay_rate / float(tokens * count)
    rates = own(jnp.repeat(rate, count // groups, axis=0))
    res = own(residue.reshape(count, cw, modes)).transpose(0, 2, 1)
    skip = own(skip_gain.reshape(count, cw))[:, None, :]
    tiled = jnp.tile(rates, (1, subs))
    rate_col, rate_row = tiled[:, :, None], tiled[:, None, :]
    powers = call(
        lambda place, *refs: powers_kernel(*refs, tokens=tokens, modes=modes),
        (blocks,),
        [block((depth, 1)), block((1, depth)), block((modes, cw))],
        [block((depth, tokens))] * 4 + [block((tokens, depth))] * 4 + [block((SUB, cw))],
        [b16(blocks, depth, tokens)] * 4 + [b16(blocks, tokens, depth)] * 4 + [f32(blocks, SUB, cw)],
        moved=blocks * depth * tokens * 16, name="powers",
    )(place, rate_col, rate_row, res)
    af, ab, lf, lb, taps = powers[0:2], powers[2:4], powers[4:6], powers[6:8], powers[8]

    ring = [out_weight, shift(out_weight, 1, True)]
    vs = {s: swap(sent[s], s) for s in (2, 3, 1)}
    vs = [sent[0]] + [vs[s] for s in range(1, LANES)]
    gates = pack(after(gating, *vs[1:]))
    gs = [gates[0]] + [swap(gates[s], s) for s in range(1, LANES)]
    cot_y = swap(after(cotangent, taps, *vs[1:]), 2)
    ring.append(shift(after(ring[-1], *vs[1:]), 1, True))

    scratch = [
        pltpu.VMEM((tokens, cw), F32),
        pltpu.VMEM((LANES, modes, cw), F32),
        pltpu.VMEM((LANES, modes, cw), F32),
    ]
    common = [block((SUB, cw)), block((modes, cw)), block((depth, 1)), block((1, cw))]
    lead = [block((tokens, depth))] * 2 + [block((modes, cw)), block((depth, 1))]
    value_part = [pl.BlockSpec((1, 1, tokens, cw), lambda i, *_: (0, i, 0, 0))] * LANES
    gate_part = [pl.BlockSpec((1, 1, tokens, cw), lambda i, *_: (0, i, 0, 0))] * LANES
    cols = lambda r: pl.BlockSpec((r, tile), lambda i, *_: (0, i))

    def scan(own_end, sign, doubling):
        fade = jnp.exp(-float(span) * rates)[:, :, None]
        total, held, hop, first = None, own_end, 1, None
        while hop < blocks:
            got = jnp.roll(shift(held.astype(BF16), sign * hop, False), sign * hop, axis=0).astype(F32)
            first = got if first is None else first
            total = got if total is None else total + fade ** (hop - 1) * got
            if doubling:
                held = held + fade**hop * got
                hop *= 2
            else:
                hop += 1
        return total, first

    inner, end = call(
        forward_kernel, (blocks,),
        value_part + [block((depth, tokens))] * 2 + [block((tokens, depth))] * 2 + common,
        [block((span, cw)), block((modes, cw))],
        [f32(blocks, span, cw), f32(blocks, modes, cw)],
        scratch, flops=blocks * 10 * depth * span * cw, moved=blocks * span * cw * 8, name="forward",
    )(place, *vs, *af, *lf, taps, res, rate_col, skip)
    cots = [cotangent, swap(after(cotangent, end), 1), cot_y, swap(after(cot_y, end), 1)]
    coming, first = scan(end, 1, True)
    ring.append(shift(after(ring[-1], first), 1, True))
    for _ in range(blocks - len(ring)):
        ring.append(shift(ring[-1], 1, True))
    conv, mixed, turned = call(
        mixed_kernel, (blocks,),
        [block((modes, cw))] + gate_part + [block((span, cw))] + lead,
        [block((span, cw)), block((span, cw)), block((cw, span))],
        [f32(blocks, span, cw), b16(blocks, span, cw), b16(blocks, cw, span)],
        flops=blocks * 6 * span * cw * modes, moved=blocks * span * cw * 14, name="mixed",
    )(place, coming, *gs, inner, *lf, res, rate_col)
    wgrads = call(
        weight_kernel, (steps,),
        [whole((blocks, cw, span))] + [cols(tokens)] * LANES,
        [cols(cw)] * blocks, [f32(cw, width)] + [b16(cw, width)] * hops,
        flops=2 * blocks * span * cw * width, moved=4 * span * width, name="weight",
    )(place, turned, *cots)
    part = shift(wgrads[-1], -1, True)

    def pass_on_sum(part, m):
        return shift((wgrads[m] + part.astype(F32)).astype(BF16), -1, True)

    keep, pass_on, send = call(
        functools.partial(output_kernel, blocks=blocks), (steps,),
        [whole((blocks, span, cw))] + [cols(cw)] * blocks,
        [cols(tokens), cols(tokens), pl.BlockSpec((2, tokens, tile), lambda i, *_: (0, 0, i))],
        [f32(tokens, width), f32(tokens, width), b16(2, tokens, width)],
        flops=2 * span * blocks * cw * width, moved=4 * width * blocks * cw, name="output",
    )(place, after(mixed, wgrads), *ring)
    near = swap(send, 1)
    far = swap((pass_on + near[1].astype(F32)).astype(BF16), 2)
    output = keep + near[0].astype(F32) + far.astype(F32)

    grad = call(
        functools.partial(grad_kernel, blocks=blocks), (steps,),
        [cols(cw)] * blocks + [cols(tokens)] * LANES,
        whole((blocks, span, cw)), f32(blocks, span, cw),
        flops=2 * blocks * span * cw * width, moved=4 * span * width, name="grad",
    )(place, *ring, *after(tuple(cots), wgrads))
    out = call(
        backward_kernel, (blocks,),
        gate_part + [block((span, cw))] * 2 + [block((depth, tokens))] * 2 + [block((tokens, depth))] * 2 + common,
        [block((tokens, cw))] * LANES + [block((span, cw)), block((modes, cw))],
        [b16(blocks, tokens, cw)] * LANES + [f32(blocks, span, cw), f32(blocks, modes, cw)],
        scratch, flops=blocks * 12 * depth * span * cw, moved=blocks * span * cw * 20, name="backward",
    )(place, *gs, after(grad, near), conv, *ab, *lb, taps, res, rate_col, skip)
    ggrads, inner_back, end_back = out[:LANES], out[LANES], out[LANES + 1]
    coming, first = scan(end_back, -1, blocks > 4)
    part = pass_on_sum(after(part, end_back), blocks - 2)

    vgrads = call(
        value_kernel, (blocks,),
        [block((modes, cw))] + [block((span, cw))] + lead,
        [block((tokens, cw))] * LANES, [b16(blocks, tokens, cw)] * LANES,
        flops=blocks * 6 * span * cw * modes, moved=blocks * 6 * span * cw, name="value",
    )(place, after(coming, far), inner_back, *lb, res, rate_col)
    for m in range(blocks - 3, 0, -1):
        part = pass_on_sum(after(part, vgrads[0]) if m == blocks - 3 else part, m)
    wgrad = wgrads[0] + part.astype(F32)
    gg = {s: swap(ggrads[s], s) for s in (2, 3, 1)}
    gg = [ggrads[0]] + [gg[s] for s in range(1, LANES)]
    vv = {s: swap(vgrads[s], s) for s in (2, 3, 1)}
    vv = [vgrads[0]] + [vv[s] for s in range(1, LANES)]
    if aligned:
        value_grad, gate_grad = call(
            functools.partial(unpack_kernel, blocks=blocks, width=cw), (1,),
            [whole((blocks, tokens, cw))] * (2 * LANES), [whole((tokens, width))] * 2,
            [b16(tokens, width)] * 2, moved=8 * tokens * width, name="unpack",
        )(place, *vv, *gg)
    else:

        def joined(pieces):
            full = by_slot(jnp.stack(by_lane(pieces), axis=1))
            return full.transpose(2, 0, 1, 3).reshape(tokens, width)

        value_grad, gate_grad = joined(vv), joined(gg)
    return output.astype(BF16), value_grad, gate_grad, wgrad


def solution(mesh):
    rows = P(("parts", "ctx"), None)
    return jax.shard_map(
        per_device,
        mesh=mesh,
        in_specs=(rows, rows, rows, P("parts", None), P("parts", None), P("parts"), rows),
        out_specs=(rows, rows, rows, rows),
        check_vma=False,
    )
```
